128 devices in a mesh: pool: 32 (over x, z, core), exp: 4 (over y).
Axes of the slice: x: 4, y: 4, z: 4, core: 2. Of those that a mesh axis runs over, the one named last changes fastest.
Arguments:
- tokens: bfloat16 [512, 1024], P('pool'), as said below
- block_table: int32 [512, 128], replicated, may hold values from -1 to 4607, as said below
- lengths: int32 [512], replicated, may hold values from 1 to 16384, as said below
- k_cache: bfloat16 [4096, 128, 512], P('pool', None, 'exp'), as said below
- v_cache: bfloat16 [4096, 128, 512], P('pool', None, 'exp'), may hold values from -9 to 9
- hidden_store: bfloat16 [512, 128, 1024], P('pool'), may hold values from -6 to 6
- norm_attn: bfloat16 [1024], replicated, may hold values from 0.5 to 1.5
- w_query: bfloat16 [1024, 1024], P(None, 'exp'), as said below
- w_key: bfloat16 [1024, 512], P(None, 'exp'), may hold values from -0.1875 to 0.1875
- w_value: bfloat16 [1024, 512], P(None, 'exp'), may hold values from -0.1875 to 0.1875
- w_out: bfloat16 [1024, 1024], P('exp'), may hold values from -0.1875 to 0.1875
- norm_moe: bfloat16 [1024], replicated, may hold values from 0.5 to 1.5
- expert_ids: int32 [512, 8], P('pool'), may hold values from 0 to 31, all different within a row; in each aligned block of 16 rows (0 to 15, 16 to 31, ...) at most 8 rows name the same one
- gate_weights: float32 [512, 8], P('pool'), may hold values from 0.1 to 1
- w_gate: bfloat16 [32, 1024, 512], P('pool'), may hold values from -0.1875 to 0.1875
- w_up: bfloat16 [32, 1024, 512], P('pool'), may hold values from -0.1875 to 0.1875
- w_down: bfloat16 [32, 512, 1024], P('pool'), may hold values from -0.25 to 0.25
Outputs:
- layer_out: bfloat16 [512, 1024], P('pool', 'exp')
The draws below stay inside these ranges and needn't reach their ends.
Inputs may be any that keep to these rules, and one draw needn't show every extreme that they name: `block_table`: every block number 0 to 4607 stands exactly once in the table; a request's blocks fill the start of its row and -1 fills the rest; each request has 1 to 128 blocks and some request has exactly 128. `lengths`: A request with n blocks has a length above (n - 1) * 128 and at most n * 128; some request has the length 16384. `expert_ids`: in the rows of one pool index no expert is named by more than 8 rows. `tokens`: entries lie within -8 to 8. `k_cache`: entries lie within -8 to 8. `w_query`: entries are of magnitude below 7 / sqrt(1024).
All inputs are finite; a program needn't handle non-finite values.
Results may differ from the reference program's by a relative error of at most 0.009.
Values may be sent and summed in bfloat16 or wider, within the bound.
No kernel may reach another device: no remote copies, remote signals or barrier semaphores. Data moves between devices by JAX's collectives and lax.ppermute only.
A program may use at most 128 MiB of HBM per device.

```python
import math
import jax
import jax.numpy as jnp
import numpy as np
from jax import lax

D = 1024
QUERY_HEADS = 16
KEY_VALUE_HEADS = 8
HEAD_SIZE = 64
FF = 512
TOP = 8
BLOCK_TOKENS = 128
REQUEST_BLOCKS = 128
REQ_DEV = 16
NB_DEV = 128
NH_DEV = 16
TOTAL_SLOTS = 4608
KV_BLOCKS = 4096
HIDDEN_BLOCKS = 512
REQUESTS = 512
EXPERTS = 32
CAP = 8
QW = 1024
KW = 512
N_POOL = 32


def table_parts(key):
    base_key = jax.random.fold_in(key, 14)
    key_heavy, key_weight, key_order, key_perm, key_tail = jax.random.split(base_key, 5)
    req_ids = jnp.arange(REQUESTS, dtype=jnp.int32)
    heavy_req = jax.random.randint(key_heavy, (), 0, REQUESTS)
    heavy_flag = req_ids == heavy_req
    draw_weight = jax.random.randint(key_weight, (REQUESTS,), 1, 3) ** 2
    draw_weight = jnp.where(heavy_flag, 0, draw_weight)
    extra_blocks = TOTAL_SLOTS - REQUEST_BLOCKS - (REQUESTS - 1)
    shared_block_list = extra_blocks * draw_weight // jnp.sum(draw_weight)
    remaining_count = extra_blocks - jnp.sum(shared_block_list)
    order_perm = jax.random.permutation(key_order, REQUESTS)
    req_rank = jnp.zeros((REQUESTS,), jnp.int32).at[order_perm].set(req_ids)
    heavy_rank = req_rank[heavy_req]
    peer_rank = req_rank - jnp.where(req_rank > heavy_rank, 1, 0)
    extra_credit = jnp.where((peer_rank < remaining_count) & jnp.logical_not(heavy_flag), 1, 0)
    token_counts = jnp.where(heavy_flag, REQUEST_BLOCKS, 1 + shared_block_list + extra_credit).astype(jnp.int32)
    offsets = jnp.cumsum(token_counts) - token_counts
    slot_perm = jax.random.permutation(key_perm, TOTAL_SLOTS).astype(jnp.int32)
    list_pos = jnp.arange(REQUEST_BLOCKS, dtype=jnp.int32)
    gather_at = jnp.clip(offsets[:, None] + list_pos[None, :], 0, TOTAL_SLOTS - 1)
    table = jnp.where(list_pos[None, :] < token_counts[:, None], slot_perm[gather_at], -1)
    tail_len = jax.random.randint(key_tail, (REQUESTS,), 1, BLOCK_TOKENS + 1)
    tail_len = jnp.where(heavy_flag, BLOCK_TOKENS, tail_len)
    length_vals = (token_counts - 1) * BLOCK_TOKENS + tail_len
    return (table.astype(jnp.int32), length_vals.astype(jnp.int32))


def draw_block_table(key, part):
    return table_parts(key)[0]


def draw_lengths(key, part):
    return table_parts(key)[1]


def draw_tokens(key, part):
    key_noise = jax.random.fold_in(jax.random.fold_in(key, 13), 0)
    noise_vals = jnp.clip(jax.random.normal(key_noise, (REQUESTS, D), jnp.float32), -6.0, 6.0)
    drawn = 0.5 * noise_vals
    return drawn.astype(jnp.bfloat16)


def draw_w_query(key, part):
    drawn = jnp.clip(jax.random.normal(jax.random.fold_in(key, 11), (D, QW), jnp.float32), -6.0, 6.0) / math.sqrt(D)
    return drawn.astype(jnp.bfloat16)


def draw_k_cache(key, part):
    base_key = jax.random.fold_in(key, 12)
    key_noise = jax.random.fold_in(base_key, 0)
    cache_shape = (KV_BLOCKS, BLOCK_TOKENS, KW)
    drawn = jnp.clip(jax.random.normal(key_noise, cache_shape, jnp.float32), -6.0, 6.0)
    return drawn.astype(jnp.bfloat16)


def steps_of(stream_key, extent, shards, low, high):
    def one(dim, parts):
        steps = jax.random.uniform(jax.random.fold_in(jax.random.fold_in(stream_key, 6), dim), (parts,), jnp.float32, low / len(shards), high / len(shards))
        return jnp.repeat(jnp.exp(steps), extent[dim] // parts).reshape((-1,) + (1,) * (len(extent) - dim - 1))

    gain = one(*shards[0])
    for cut in shards[1:]:
        gain = gain * one(*cut)
    return gain


def routed_block(own_key, own, number, rows, count, top, most, slope):
    sequence = jax.random.permutation(own_key, count)
    heavy_load, ordinary = portions_of(count, rows * top, most, slope, True), portions_of(count, rows * top, most, slope, False)
    places = jnp.arange(count)

    def named(sizes, offset_by):
        used = int((sizes > 0).sum())
        fixed = max(1, used // 4)
        moved = fixed + (places - fixed + offset_by * (used - fixed)) % max(1, count - fixed)
        return jnp.zeros((count,), jnp.int32).at[sequence[jnp.where(places < fixed, places, moved)]].set(jnp.asarray(sizes, jnp.int32))

    sizes = jnp.where(number % 4 == 0, named(heavy_load, number // 4), named(ordinary, number - number // 4 - 1))
    mixed = jax.random.permutation(jax.random.fold_in(own, 3), count)
    donor, taker = mixed[0:count // 2 * 2:2], mixed[1:count // 2 * 2:2]
    slack = jnp.minimum(sizes[donor] - 1, most - sizes[taker]) // 2
    slack = jnp.where((donor == sequence[0]) | (taker == sequence[0]) | (sizes[taker] == 0), 0, jnp.maximum(slack, 0))
    moved = jax.random.randint(jax.random.fold_in(own, 4), (count // 2,), 0, 1 << 20) % (slack + 1)
    sizes = sizes.at[donor].add(-moved).at[taker].add(moved)
    labels = jnp.searchsorted(jnp.cumsum(sizes), jnp.arange(rows * top), side="right").astype(jnp.int32)
    table = labels.reshape(top, rows).T
    table = table[jax.random.permutation(jax.random.fold_in(own, 1), rows)]
    offset_by = jax.random.randint(jax.random.fold_in(own, 2), (rows, 1), 0, top)
    return jnp.take_along_axis(table, (jnp.arange(top)[None, :] + offset_by) % top, axis=1)


def portions_of(amount, total, most, slope, full):
    loads = [(1 << 20) // math.isqrt(rank ** slope) + 1 for rank in range(1, amount + 1)]
    largest = most if full else min(most, max(-(-total // amount), total * loads[0] // sum(loads)))
    least = 1 if total - largest >= amount - 1 else 0
    holding, surplus = [largest] + [least] * (amount - 1), total - largest - least * (amount - 1)
    while surplus > 0:
        movable = [i for i in range(1, amount) if holding[i] < largest] or [i for i in range(1, amount) if holding[i] < most]
        mass, remaining = sum([loads[i] for i in movable]), surplus
        for i in movable:
            extra = min(most - holding[i], max(1, remaining * loads[i] // mass), surplus)
            holding[i] = holding[i] + extra
            surplus = surplus - extra
    return np.array(holding)


def scatter_about(own_key, shape, deviation, most, shards=(), kind=jnp.bfloat16):
    values = jax.random.normal(own_key, shape, jnp.float32) * deviation
    if len(shards) > 0:
        values = steps_of(own_key, shape, shards, -0.22, 0.18) * values
    return jnp.clip(values, min=-most, max=most).astype(kind)


def setup_inputs(seed: int = 0) -> dict:
    keys = jax.random.split(jax.random.key(seed), 18)
    tokens = draw_tokens(jax.random.fold_in(keys[17], 71), 0)
    block_table = draw_block_table(jax.random.fold_in(keys[17], 71), 0)
    lengths = draw_lengths(jax.random.fold_in(keys[17], 71), 0)
    k_cache = draw_k_cache(jax.random.fold_in(keys[17], 71), 0)
    v_cache = scatter_about(keys[4], (KV_BLOCKS, BLOCK_TOKENS, KW), 1.5, 9.0, ((0, 32), (2, 4)))
    hidden_store = scatter_about(keys[5], (HIDDEN_BLOCKS, BLOCK_TOKENS, D), 1.0, 6.0, ((0, 32),))
    norm_attn = jnp.clip(1.0 + 0.1 * jax.random.normal(keys[6], (D,), jnp.float32), 0.5, 1.5).astype(jnp.bfloat16)
    w_query = draw_w_query(jax.random.fold_in(keys[17], 71), 0)
    w_key = scatter_about(keys[8], (D, KW), D ** -0.5, 0.1875, ((1, 4),))
    w_value = scatter_about(keys[9], (D, KW), D ** -0.5, 0.1875, ((1, 4),))
    w_out = scatter_about(keys[10], (QW, D), QW ** -0.5, 0.1875, ((0, 4),))
    norm_moe = jnp.clip(1.0 + 0.1 * jax.random.normal(keys[11], (D,), jnp.float32), 0.5, 1.5).astype(jnp.bfloat16)
    expert_ids_keys = jax.random.split(jax.random.fold_in(keys[12], 1), REQUESTS // REQ_DEV)
    expert_ids_turns = jax.random.permutation(jax.random.fold_in(keys[12], 3), REQUESTS // REQ_DEV)
    expert_ids = jax.vmap(lambda own, number: routed_block(jax.random.fold_in(keys[12], 2), own, number, REQ_DEV, EXPERTS, TOP, CAP, 2))(expert_ids_keys, expert_ids_turns).reshape((REQUESTS, TOP))
    gate_weights = jnp.clip(jnp.exp(math.log(1.0) - 2.3025851 * jax.random.uniform(keys[13], (REQUESTS, TOP), jnp.float32) ** steps_of(keys[13], (REQUESTS, TOP), ((0, 32),), -0.2, 0.2)), 0.1, 1.0)
    w_gate = scatter_about(keys[14], (EXPERTS, D, FF), D ** -0.5, 0.1875, ((0, 32),))
    w_up = scatter_about(keys[15], (EXPERTS, D, FF), D ** -0.5, 0.1875, ((0, 32),))
    w_down = scatter_about(keys[16], (EXPERTS, FF, D), FF ** -0.5, 0.25, ((0, 32),))
    return {"tokens": tokens, "block_table": block_table, "lengths": lengths, "k_cache": k_cache, "v_cache": v_cache, "hidden_store": hidden_store, "norm_attn": norm_attn, "w_query": w_query, "w_key": w_key, "w_value": w_value, "w_out": w_out, "norm_moe": norm_moe, "expert_ids": expert_ids, "gate_weights": gate_weights, "w_gate": w_gate, "w_up": w_up, "w_down": w_down}


NEG_FILL = -1e+30
EPSILON = 1e-05
SCORE_SCALE = 0.125

def rms_scale(row_vals, gain_row):
    mean_sq = lax.optimization_barrier(jnp.mean(row_vals * row_vals, axis=-1, keepdims=True))
    return row_vals * lax.rsqrt(mean_sq + EPSILON) * gain_row

def reference(tokens, block_table, lengths, k_cache, v_cache, hidden_store, norm_attn, w_query, w_key, w_value, w_out, norm_moe, expert_ids, gate_weights, w_gate, w_up, w_down):
    x_rows = tokens.astype(jnp.float32)
    normed = rms_scale(x_rows, norm_attn.astype(jnp.float32)).astype(jnp.bfloat16)
    queries = jnp.dot(normed, w_query, preferred_element_type=jnp.float32).astype(jnp.bfloat16)
    stored_rows = hidden_store.reshape(-1, D)
    key_new = jnp.dot(stored_rows, w_key, preferred_element_type=jnp.float32).astype(jnp.bfloat16)
    value_new = jnp.dot(stored_rows, w_value, preferred_element_type=jnp.float32).astype(jnp.bfloat16)
    every_key = jnp.concatenate([k_cache.reshape(N_POOL, NB_DEV, BLOCK_TOKENS, KW), key_new.reshape(N_POOL, NH_DEV, BLOCK_TOKENS, KW)], axis=1).reshape(TOTAL_SLOTS, BLOCK_TOKENS, KW)
    every_value = jnp.concatenate([v_cache.reshape(N_POOL, NB_DEV, BLOCK_TOKENS, KW), value_new.reshape(N_POOL, NH_DEV, BLOCK_TOKENS, KW)], axis=1).reshape(TOTAL_SLOTS, BLOCK_TOKENS, KW)
    group_width = QUERY_HEADS // KEY_VALUE_HEADS

    def one_request(packed):
        table_row, length, query_row = packed
        selected_entries = jnp.clip(table_row, 0, TOTAL_SLOTS - 1)
        key_block_list = every_key[selected_entries].reshape(REQUEST_BLOCKS, BLOCK_TOKENS, KEY_VALUE_HEADS, HEAD_SIZE).astype(jnp.float32)
        value_block_list = every_value[selected_entries].reshape(REQUEST_BLOCKS, BLOCK_TOKENS, KEY_VALUE_HEADS, HEAD_SIZE).astype(jnp.float32)
        query_head_rows = query_row.reshape(KEY_VALUE_HEADS, group_width, HEAD_SIZE).astype(jnp.float32)
        scores = jnp.einsum('gqd,btgd->bgqt', query_head_rows, key_block_list) * SCORE_SCALE
        positions = jnp.arange(REQUEST_BLOCKS)[:, None] * BLOCK_TOKENS + jnp.arange(BLOCK_TOKENS)[None, :]
        is_valid = (positions < length) & (table_row >= 0)[:, None]
        is_valid = is_valid[:, None, None, :]
        masked = jnp.where(is_valid, scores, NEG_FILL)
        block_top = lax.optimization_barrier(jnp.max(masked, axis=-1))
        weights = jnp.where(is_valid, jnp.exp(masked - block_top[..., None]), 0.0)
        block_sum = lax.optimization_barrier(jnp.sum(weights, axis=-1))
        weight_low = lax.optimization_barrier(weights.astype(jnp.bfloat16)).astype(jnp.float32)
        block_out = jnp.einsum('bgqt,btgd->bgqd', weight_low, value_block_list)
        row_top = lax.optimization_barrier(jnp.max(block_top, axis=0))
        factor = jnp.exp(block_top - row_top[None])
        total_sum = lax.optimization_barrier(jnp.sum(block_sum * factor, axis=0))
        accum = lax.optimization_barrier(jnp.sum(block_out * factor[..., None], axis=0))
        return (accum / total_sum[..., None]).reshape(QW)
    attended = lax.map(one_request, (block_table, lengths, queries)).astype(jnp.bfloat16)
    projected = jnp.dot(attended, w_out, preferred_element_type=jnp.float32)
    mixed = x_rows + projected
    normed_moe = rms_scale(mixed, norm_moe.astype(jnp.float32)).astype(jnp.bfloat16)

    def add_expert(running, expert_index):
        gate_act = jnp.dot(normed_moe, w_gate[expert_index], preferred_element_type=jnp.float32)
        up_act = jnp.dot(normed_moe, w_up[expert_index], preferred_element_type=jnp.float32)
        hidden = (jax.nn.silu(gate_act) * up_act).astype(jnp.bfloat16)
        expert_low = jnp.dot(hidden, w_down[expert_index], preferred_element_type=jnp.float32).astype(jnp.bfloat16)
        expert_out = lax.optimization_barrier(expert_low).astype(jnp.float32)
        coeff = lax.optimization_barrier(jnp.sum(jnp.where(expert_ids == expert_index, gate_weights, 0.0), axis=1))
        return (running + coeff[:, None] * expert_out, None)
    moe_out, _ = lax.scan(add_expert, jnp.zeros((REQUESTS, D), jnp.float32), jnp.arange(EXPERTS))
    return (mixed + moe_out).astype(jnp.bfloat16)
```

```python
import jax
import jax.numpy as jnp
from jax import lax
from jax.sharding import PartitionSpec as P

HEAD_SIZE = 64


NEG_FILL = -1e30
EPSILON = 1e-05
SCORE_SCALE = 0.125
HIGHEST = lax.Precision.HIGHEST


def gather_pool(value):
    copies = jnp.broadcast_to(value[None], (lax.axis_size("pool"),) + value.shape)
    return lax.all_to_all(copies, "pool", split_axis=0, concat_axis=0, tiled=True)


def sum_exp(value):
    size = lax.axis_size("exp")
    if size != 4:
        return lax.psum(value, "exp")
    value = value + lax.ppermute(value, "exp", [(0, 1), (1, 0), (2, 3), (3, 2)])
    return value + lax.ppermute(value, "exp", [(0, 3), (3, 0), (1, 2), (2, 1)])


def split_three(value):
    high = lax.reduce_precision(value, 8, 7)
    rest = value - high
    middle = lax.reduce_precision(rest, 8, 7)
    return [part.astype(jnp.bfloat16) for part in (high, middle, rest - middle)]


def rms_scale(row_vals, gain_row):
    mean_sq = jnp.mean(row_vals * row_vals, axis=-1, keepdims=True)
    return row_vals * lax.rsqrt(mean_sq + EPSILON) * gain_row


def on_device(
    tokens,
    block_table,
    lengths,
    k_cache,
    v_cache,
    hidden_store,
    norm_attn,
    w_query,
    w_key,
    w_value,
    w_out,
    norm_moe,
    expert_ids,
    gate_weights,
    w_gate,
    w_up,
    w_down,
):
    pool_count = lax.axis_size("pool")
    exp_count = lax.axis_size("exp")
    pool_index = lax.axis_index("pool")
    exp_index = lax.axis_index("exp")
    req_dev = tokens.shape[0]
    model_width = tokens.shape[1]
    quarter = model_width // exp_count
    x_rows = tokens.astype(jnp.float32)
    normed = rms_scale(x_rows, norm_attn.astype(jnp.float32)).astype(jnp.bfloat16)
    queries = jnp.dot(normed, w_query, preferred_element_type=jnp.float32).astype(jnp.bfloat16)
    all_queries = gather_pool(queries).reshape(-1, queries.shape[1])
    stored_rows = hidden_store.reshape(-1, model_width)
    stored_shape = (hidden_store.shape[0], hidden_store.shape[1], w_key.shape[1])
    key_new = (
        jnp.dot(stored_rows, w_key, preferred_element_type=jnp.float32)
        .astype(jnp.bfloat16)
        .reshape(stored_shape)
    )
    value_new = (
        jnp.dot(stored_rows, w_value, preferred_element_type=jnp.float32)
        .astype(jnp.bfloat16)
        .reshape(stored_shape)
    )
    keys_here = jnp.concatenate([k_cache, key_new], axis=0)
    values_here = jnp.concatenate([v_cache, value_new], axis=0)
    slot_count, page_len, key_width = keys_here.shape
    query_width = queries.shape[1]
    kv_groups = key_width // HEAD_SIZE
    per_group = query_width // key_width
    head_count = query_width // HEAD_SIZE
    requests = block_table.shape[0]
    list_len = block_table.shape[1]
    flat_ids = block_table.reshape(-1)
    entry_index = jnp.arange(requests * list_len, dtype=jnp.int32)
    global_slot = pool_index * slot_count + jnp.arange(slot_count, dtype=jnp.int32)
    found_entry = jnp.sum(
        jnp.where(flat_ids[None, :] == global_slot[:, None], entry_index[None, :], 0), axis=1
    )
    slot_req = found_entry // list_len
    slot_block = found_entry % list_len
    member = slot_req[:, None] == jnp.arange(requests, dtype=jnp.int32)[None, :]
    member_low = member.astype(jnp.bfloat16)
    slot_queries = jnp.dot(member_low, all_queries, preferred_element_type=jnp.float32).astype(
        jnp.bfloat16
    )
    slot_length = jnp.sum(jnp.where(member, lengths[None, :], 0), axis=1)
    q_grouped = slot_queries.reshape(slot_count, kv_groups, per_group, HEAD_SIZE)
    k_grouped = keys_here.reshape(slot_count, page_len, kv_groups, HEAD_SIZE)
    v_grouped = values_here.reshape(slot_count, page_len, kv_groups, HEAD_SIZE)
    scores = (
        jnp.einsum("sgqd,stgd->sgqt", q_grouped, k_grouped, preferred_element_type=jnp.float32)
        * SCORE_SCALE
    )
    positions = slot_block[:, None] * page_len + jnp.arange(page_len, dtype=jnp.int32)[None, :]
    is_valid = (positions < slot_length[:, None])[:, None, None, :]
    masked = jnp.where(is_valid, scores, NEG_FILL)
    block_top = jnp.max(masked, axis=-1)
    weights = jnp.where(is_valid, jnp.exp(masked - block_top[..., None]), 0.0)
    block_sum = jnp.sum(weights, axis=-1)
    block_out = jnp.einsum(
        "sgqt,stgd->sgqd",
        weights.astype(jnp.bfloat16),
        v_grouped,
        preferred_element_type=jnp.float32,
    )
    slot_top = block_top.reshape(slot_count, head_count)
    slot_sum = block_sum.reshape(slot_count, head_count)
    slot_out = block_out.reshape(slot_count, query_width)
    local_top = jnp.max(jnp.where(member[:, :, None], slot_top[:, None, :], NEG_FILL), axis=0)
    own_top = jnp.max(jnp.where(member[:, :, None], local_top[None, :, :], NEG_FILL), axis=1)
    factor = jnp.exp(slot_top - own_top)
    one_hot = member.astype(jnp.float32)
    local_sum = jnp.einsum("sr,sh->rh", one_hot, slot_sum * factor, precision=HIGHEST)
    scaled_out = (slot_out * jnp.repeat(factor, HEAD_SIZE, axis=1)).astype(jnp.bfloat16)
    local_out = jnp.einsum(
        "sr,sc->rc", member_low, scaled_out, preferred_element_type=jnp.float32
    ).astype(jnp.bfloat16)
    pieces = split_three(local_top) + split_three(local_sum)
    parcel = jnp.concatenate([local_out] + pieces, axis=1)
    parcel = jnp.pad(parcel, ((0, 0), (0, -parcel.shape[1] % 128)))
    parcel = parcel.reshape(pool_count, req_dev, -1)
    landed = lax.all_to_all(parcel, "pool", split_axis=0, concat_axis=0, tiled=True)
    part_out = landed[:, :, :query_width].astype(jnp.float32)
    part_stats = landed[:, :, query_width : query_width + 6 * head_count].astype(jnp.float32)
    part_stats = part_stats.reshape(pool_count, req_dev, 2, 3, head_count)
    part_stats = part_stats[:, :, :, 0] + part_stats[:, :, :, 1] + part_stats[:, :, :, 2]
    part_top = part_stats[:, :, 0]
    part_weight = jnp.exp(part_top - jnp.max(part_top, axis=0, keepdims=True))
    total_sum = jnp.sum(part_weight * part_stats[:, :, 1], axis=0)
    accum = jnp.sum(part_out * jnp.repeat(part_weight, HEAD_SIZE, axis=-1), axis=0)
    attended = (accum / jnp.repeat(total_sum, HEAD_SIZE, axis=-1)).astype(jnp.bfloat16)
    projected = sum_exp(jnp.dot(attended, w_out, preferred_element_type=jnp.float32))
    mixed = x_rows + projected
    normed_moe = rms_scale(mixed, norm_moe.astype(jnp.float32)).astype(jnp.bfloat16)
    top_count = expert_ids.shape[1]
    capacity = min(req_dev, 2 * ((req_dev * top_count + pool_count - 1) // pool_count))
    route_flat = expert_ids.reshape(-1)
    expert_hit = (route_flat[:, None] == jnp.arange(pool_count, dtype=jnp.int32)[None, :]).astype(
        jnp.int32
    )
    slot_rank = jnp.sum(jnp.cumsum(expert_hit, axis=0) * expert_hit, axis=1) - 1
    slot_pos = route_flat * capacity + slot_rank
    placed = (
        slot_pos[:, None] == jnp.arange(pool_count * capacity, dtype=jnp.int32)[None, :]
    ).astype(jnp.float32)
    placed = placed.reshape(req_dev, top_count, pool_count * capacity)
    send_map = jnp.sum(placed, axis=1).astype(jnp.bfloat16)
    combine_map = jnp.einsum("tk,tkc->tc", gate_weights, placed, precision=HIGHEST)
    outgoing = jnp.einsum("tc,td->cd", send_map, normed_moe, preferred_element_type=jnp.float32)
    outgoing = outgoing.astype(jnp.bfloat16).reshape(pool_count, capacity, model_width)
    arrived = lax.all_to_all(outgoing, "pool", split_axis=0, concat_axis=0, tiled=True)
    sources = arrived.shape[0]
    slots_here = arrived.shape[1]
    row_block = arrived.reshape(-1, model_width)
    gate_act = jnp.dot(row_block, w_gate[0], preferred_element_type=jnp.float32)
    up_act = jnp.dot(row_block, w_up[0], preferred_element_type=jnp.float32)
    hidden = (jax.nn.silu(gate_act) * up_act).astype(jnp.bfloat16)
    expert_low = jnp.dot(hidden, w_down[0], preferred_element_type=jnp.float32).astype(jnp.bfloat16)
    expert_low = expert_low.reshape(sources, slots_here, model_width)
    expert_out = lax.dynamic_slice_in_dim(expert_low, exp_index * quarter, quarter, 2)
    returned = lax.all_to_all(expert_out, "pool", split_axis=0, concat_axis=0, tiled=True)
    moe_share = jnp.dot(
        combine_map,
        returned.reshape(pool_count * capacity, quarter).astype(jnp.float32),
        precision=HIGHEST,
    )
    mixed_share = lax.dynamic_slice_in_dim(mixed, exp_index * quarter, quarter, 1)
    return (mixed_share + moe_share).astype(jnp.bfloat16)


def solution(mesh):
    placed = (
        P("pool", None),
        P(),
        P(),
        P("pool", None, "exp"),
        P("pool", None, "exp"),
        P("pool", None, None),
        P(),
        P(None, "exp"),
        P(None, "exp"),
        P(None, "exp"),
        P("exp", None),
        P(),
        P("pool", None),
        P("pool", None),
        P("pool", None, None),
        P("pool", None, None),
        P("pool", None, None),
    )
    return jax.shard_map(
        on_device, mesh=mesh, in_specs=placed, out_specs=P("pool", "exp"), check_vma=False
    )
```

```python
import jax
import jax.numpy as jnp
from jax import lax
from jax.experimental import pallas as pl
from jax.experimental.pallas import tpu as pltpu
from jax.sharding import PartitionSpec as P

HEAD_SIZE = 64


NEG_FILL = -1e30
EPSILON = 1e-05
SCORE_SCALE = 0.125
HIGHEST = lax.Precision.HIGHEST


def gather_pool(value):
    copies = jnp.broadcast_to(value[None], (lax.axis_size("pool"),) + value.shape)
    return lax.all_to_all(copies, "pool", split_axis=0, concat_axis=0, tiled=True)


def sum_exp(value):
    size = lax.axis_size("exp")
    if size != 4:
        return lax.psum(value, "exp")
    value = value + lax.ppermute(value, "exp", [(0, 1), (1, 0), (2, 3), (3, 2)])
    return value + lax.ppermute(value, "exp", [(0, 3), (3, 0), (1, 2), (2, 1)])


def split_three(value):
    high = value.astype(jnp.bfloat16).astype(jnp.float32)
    rest = value - high
    middle = rest.astype(jnp.bfloat16).astype(jnp.float32)
    return high, middle, rest - middle


HEADS = 4
QUAD = 4
ROWS = HEADS * QUAD
CHUNK = 64


def attend_kernel(k_ref, v_ref, kn_ref, vn_ref, q_ref, cols_ref, req_ref, out_ref, qs, sc, ob, cb):
    rows, page_len = sc.shape
    requests = q_ref.shape[0]
    half = page_len // 2
    old_quads = k_ref.shape[0] // QUAD
    quads = rows // ROWS

    def head_of(shape):
        return lax.broadcasted_iota(jnp.int32, shape, 0) % HEADS

    def lane_of(shape):
        return lax.broadcasted_iota(jnp.int32, shape, 1)

    for c in range(rows // CHUNK):
        at = slice(c * CHUNK, (c + 1) * CHUNK)
        hit = cols_ref[at, 0:1] == lane_of((CHUNK, requests))
        picked = jnp.dot(
            jnp.where(hit, 1.0, 0.0).astype(jnp.bfloat16),
            q_ref[...],
            preferred_element_type=jnp.float32,
        )
        low, high = picked[:, :page_len], picked[:, page_len:]
        head = head_of((CHUNK, page_len))
        first = lane_of((CHUNK, page_len)) < half
        near = jnp.where(head == 0, low, pltpu.roll(low, half, 1))
        far = jnp.where(head == 2, pltpu.roll(high, half, 1), high)
        keep = first == (head < 2)
        qs[at, :] = jnp.where(keep, jnp.where(head < 2, near, far), 0.0).astype(jnp.bfloat16)

    quad_row = lax.broadcasted_iota(jnp.int32, (ROWS, page_len), 0) // HEADS

    def score(i, keys):
        q16 = qs[pl.ds(pl.multiple_of(i * ROWS, ROWS), ROWS), :]
        wide = lax.dot_general(
            q16,
            keys.reshape(QUAD * page_len, page_len),
            (((1,), (1,)), ((), ())),
            preferred_element_type=jnp.float32,
        )
        got = wide[:, :page_len]
        for n in range(1, QUAD):
            got = jnp.where(quad_row == n, wide[:, n * page_len : (n + 1) * page_len], got)
        sc[pl.ds(pl.multiple_of(i * ROWS, ROWS), ROWS), :] = got * SCORE_SCALE

    @pl.loop(0, old_quads, step=4)
    def _(i):
        for n in range(4):
            score(i + n, k_ref[pl.ds((i + n) * QUAD, QUAD)])

    for i in range(old_quads, quads):
        score(i, kn_ref[(i - old_quads) * QUAD : (i - old_quads + 1) * QUAD])

    tops, sums = [], []
    ceiling = jnp.full((8, requests), NEG_FILL, jnp.float32)
    for c in range(rows // CHUNK):
        at = slice(c * CHUNK, (c + 1) * CHUNK)
        valid = lane_of((CHUNK, page_len)) < cols_ref[at, 1:2]
        masked = jnp.where(valid, sc[at, :], NEG_FILL)
        top = jnp.max(masked, axis=1, keepdims=True)
        weight = jnp.where(valid, jnp.exp(masked - top), 0.0)
        sc[at, :] = weight
        tops.append(top)
        sums.append(jnp.sum(weight, axis=1, keepdims=True))
        hit = cols_ref[at, 0:1] == lane_of((CHUNK, requests))
        spread = jnp.where(hit, top, NEG_FILL).reshape(CHUNK // 8, 8, requests)
        ceiling = jnp.maximum(ceiling, jnp.max(spread, axis=0))
    ceiling = jnp.maximum(ceiling, pltpu.roll(ceiling, HEADS, 0))

    def blend(i, values):
        p16 = sc[pl.ds(pl.multiple_of(i * ROWS, ROWS), ROWS), :]
        parts = [jnp.where(quad_row == n, p16, 0.0) for n in range(QUAD)]
        sc[pl.ds(pl.multiple_of(i * ROWS, ROWS), ROWS), :] = jnp.dot(
            jnp.concatenate(parts, axis=1).astype(jnp.bfloat16),
            values.reshape(QUAD * page_len, page_len),
            preferred_element_type=jnp.float32,
        )

    @pl.loop(0, old_quads, step=4)
    def _(i):
        for n in range(4):
            blend(i + n, v_ref[pl.ds((i + n) * QUAD, QUAD)])

    for i in range(old_quads, quads):
        blend(i, vn_ref[(i - old_quads) * QUAD : (i - old_quads + 1) * QUAD])

    ob[rows:, :] = jnp.zeros((ob.shape[0] - rows, ob.shape[1]), ob.dtype)
    cb[rows:, :] = jnp.zeros((cb.shape[0] - rows, cb.shape[1]), cb.dtype)
    for c in range(rows // CHUNK):
        at = slice(c * CHUNK, (c + 1) * CHUNK)
        hit = cols_ref[at, 0:1] == lane_of((CHUNK, requests))
        limit = jnp.broadcast_to(ceiling[None], (CHUNK // 8, 8, requests))
        own = jnp.max(
            jnp.where(hit, limit.reshape(CHUNK, requests), NEG_FILL), axis=1, keepdims=True
        )
        factor = jnp.exp(tops[c] - own)
        value = sc[at, :] * factor
        turned = pltpu.roll(value, half, 1)
        head = head_of((CHUNK, page_len))
        lane = lane_of((CHUNK, page_len))
        first = lane < half
        low = jnp.where(first, jnp.where(head == 0, value, 0.0), jnp.where(head == 1, turned, 0.0))
        high = jnp.where(first, jnp.where(head == 2, turned, 0.0), jnp.where(head == 3, value, 0.0))
        ob[at, :page_len] = low.astype(jnp.bfloat16)
        ob[at, page_len:] = high.astype(jnp.bfloat16)
        stats = jnp.zeros((CHUNK, page_len), jnp.float32)
        leader = jnp.where(cols_ref[at, 2:3] > 0, own, 0.0)
        pieces = split_three(sums[c] * factor) + split_three(leader)
        for n, piece in enumerate(pieces):
            stats = jnp.where(lane == n * HEADS + head, piece, stats)
        cb[at, :] = stats.astype(jnp.bfloat16)

    step = requests // 4
    for c in range(4):
        at = slice(c * step, (c + 1) * step)
        owner = lax.broadcasted_iota(jnp.int32, (step, ob.shape[0]), 0) + c * step
        member = jnp.where(owner == req_ref[0:1, :], 1.0, 0.0).astype(jnp.bfloat16)
        total = jnp.dot(member, ob[...], preferred_element_type=jnp.float32)
        out_ref[at, : 2 * page_len] = total.astype(jnp.bfloat16)
        stats = jnp.dot(member, cb[...], preferred_element_type=jnp.float32)
        lane = lane_of((step, page_len))
        joined = (
            stats
            + pltpu.roll(stats, page_len - HEADS, 1)
            + pltpu.roll(stats, page_len - 2 * HEADS, 1)
        )
        high, middle, rest = split_three(joined)
        middle, rest = pltpu.roll(middle, HEADS, 1), pltpu.roll(rest, 2 * HEADS, 1)
        stats = jnp.where(lane < 3 * HEADS, rest, stats)
        stats = jnp.where(lane < 2 * HEADS, middle, stats)
        stats = jnp.where(lane < HEADS, high, stats)
        out_ref[at, 2 * page_len :] = stats.astype(jnp.bfloat16)


def attend(k_cache, v_cache, key_new, value_new, all_queries, columns, owner_row):
    slots = k_cache.shape[0] + key_new.shape[0]
    page_len, width = k_cache.shape[1:]
    rows = slots * HEADS
    padded = owner_row.shape[1]
    requests = all_queries.shape[0]
    return pl.pallas_call(
        attend_kernel,
        out_shape=jax.ShapeDtypeStruct((requests, 3 * width), jnp.bfloat16),
        in_specs=[pl.BlockSpec(memory_space=pltpu.VMEM)] * 7,
        out_specs=pl.BlockSpec(memory_space=pltpu.VMEM),
        scratch_shapes=[
            pltpu.VMEM((rows, width), jnp.bfloat16),
            pltpu.VMEM((rows, page_len), jnp.float32),
            pltpu.VMEM((padded, 2 * width), jnp.bfloat16),
            pltpu.VMEM((padded, width), jnp.bfloat16),
        ],
        compiler_params=pltpu.CompilerParams(vmem_limit_bytes=40 << 20),
        cost_estimate=pl.CostEstimate(
            flops=4 * slots * ROWS * page_len * width * 4,
            bytes_accessed=4 * slots * page_len * width + (2 << 20),
            transcendentals=rows * page_len,
        ),
        name="attend",
    )(k_cache, v_cache, key_new, value_new, all_queries, columns, owner_row)


def rms_scale(row_vals, gain_row):
    mean_sq = jnp.mean(row_vals * row_vals, axis=-1, keepdims=True)
    return row_vals * lax.rsqrt(mean_sq + EPSILON) * gain_row


def on_device(
    tokens,
    block_table,
    lengths,
    k_cache,
    v_cache,
    hidden_store,
    norm_attn,
    w_query,
    w_key,
    w_value,
    w_out,
    norm_moe,
    expert_ids,
    gate_weights,
    w_gate,
    w_up,
    w_down,
):
    pool_count = lax.axis_size("pool")
    exp_count = lax.axis_size("exp")
    pool_index = lax.axis_index("pool")
    exp_index = lax.axis_index("exp")
    req_dev = tokens.shape[0]
    model_width = tokens.shape[1]
    quarter = model_width // exp_count
    x_rows = tokens.astype(jnp.float32)
    normed = rms_scale(x_rows, norm_attn.astype(jnp.float32)).astype(jnp.bfloat16)
    queries = jnp.dot(normed, w_query, preferred_element_type=jnp.float32).astype(jnp.bfloat16)
    all_queries = gather_pool(queries).reshape(-1, queries.shape[1])
    stored_rows = hidden_store.reshape(-1, model_width)
    stored_shape = (hidden_store.shape[0], hidden_store.shape[1], w_key.shape[1])
    key_new = (
        jnp.dot(stored_rows, w_key, preferred_element_type=jnp.float32)
        .astype(jnp.bfloat16)
        .reshape(stored_shape)
    )
    value_new = (
        jnp.dot(stored_rows, w_value, preferred_element_type=jnp.float32)
        .astype(jnp.bfloat16)
        .reshape(stored_shape)
    )
    slot_count = k_cache.shape[0] + key_new.shape[0]
    page_len = k_cache.shape[1]
    query_width = queries.shape[1]
    head_count = query_width // HEAD_SIZE
    requests = block_table.shape[0]
    list_len = block_table.shape[1]
    flat_ids = block_table.reshape(-1)
    entry_index = jnp.arange(requests * list_len, dtype=jnp.int32)
    global_slot = pool_index * slot_count + jnp.arange(slot_count, dtype=jnp.int32)
    found_entry = jnp.sum(
        jnp.where(flat_ids[None, :] == global_slot[:, None], entry_index[None, :], 0), axis=1
    )
    slot_req = found_entry // list_len
    slot_block = found_entry % list_len
    member = slot_req[:, None] == jnp.arange(requests, dtype=jnp.int32)[None, :]
    slot_length = jnp.sum(jnp.where(member, lengths[None, :], 0), axis=1)
    slot_ids = jnp.arange(slot_count, dtype=jnp.int32)
    earlier = (slot_req[:, None] == slot_req[None, :]) & (slot_ids[None, :] < slot_ids[:, None])
    leads = 1 - jnp.max(earlier.astype(jnp.int32), axis=1)
    columns = jnp.stack([slot_req, slot_length - slot_block * page_len, leads], axis=1)
    columns = jnp.repeat(columns, head_count, axis=0)
    owner_row = jnp.pad(
        jnp.repeat(slot_req, head_count), (0, -slot_count * head_count % 128), constant_values=-1
    )[None, :]
    parcel = attend(k_cache, v_cache, key_new, value_new, all_queries, columns, owner_row)
    parcel = parcel.reshape(pool_count, req_dev, -1)
    landed = lax.all_to_all(parcel, "pool", split_axis=0, concat_axis=0, tiled=True)
    part_out = landed[:, :, :query_width].astype(jnp.float32)
    part_stats = landed[:, :, query_width : query_width + 6 * head_count].astype(jnp.float32)
    part_stats = part_stats.reshape(pool_count, req_dev, 2, 3, head_count)
    part_stats = part_stats[:, :, :, 0] + part_stats[:, :, :, 1] + part_stats[:, :, :, 2]
    part_sum = part_stats[:, :, 0]
    part_top = jnp.where(part_sum > 0.0, part_stats[:, :, 1], NEG_FILL)
    part_weight = jnp.exp(part_top - jnp.max(part_top, axis=0, keepdims=True))
    total_sum = jnp.sum(part_weight * part_sum, axis=0)
    accum = jnp.sum(part_out * jnp.repeat(part_weight, HEAD_SIZE, axis=-1), axis=0)
    attended = (accum / jnp.repeat(total_sum, HEAD_SIZE, axis=-1)).astype(jnp.bfloat16)
    projected = sum_exp(jnp.dot(attended, w_out, preferred_element_type=jnp.float32))
    mixed = x_rows + projected
    normed_moe = rms_scale(mixed, norm_moe.astype(jnp.float32)).astype(jnp.bfloat16)
    top_count = expert_ids.shape[1]
    capacity = min(req_dev, 2 * ((req_dev * top_count + pool_count - 1) // pool_count))
    route_flat = expert_ids.reshape(-1)
    expert_hit = (route_flat[:, None] == jnp.arange(pool_count, dtype=jnp.int32)[None, :]).astype(
        jnp.int32
    )
    slot_rank = jnp.sum(jnp.cumsum(expert_hit, axis=0) * expert_hit, axis=1) - 1
    slot_pos = route_flat * capacity + slot_rank
    placed = (
        slot_pos[:, None] == jnp.arange(pool_count * capacity, dtype=jnp.int32)[None, :]
    ).astype(jnp.float32)
    placed = placed.reshape(req_dev, top_count, pool_count * capacity)
    send_map = jnp.sum(placed, axis=1).astype(jnp.bfloat16)
    combine_map = jnp.einsum("tk,tkc->tc", gate_weights, placed, precision=HIGHEST)
    outgoing = jnp.einsum("tc,td->cd", send_map, normed_moe, preferred_element_type=jnp.float32)
    outgoing = outgoing.astype(jnp.bfloat16).reshape(pool_count, capacity, model_width)
    arrived = lax.all_to_all(outgoing, "pool", split_axis=0, concat_axis=0, tiled=True)
    sources = arrived.shape[0]
    slots_here = arrived.shape[1]
    row_block = arrived.reshape(-1, model_width)
    gate_act = jnp.dot(row_block, w_gate[0], preferred_element_type=jnp.float32)
    up_act = jnp.dot(row_block, w_up[0], preferred_element_type=jnp.float32)
    hidden = (jax.nn.silu(gate_act) * up_act).astype(jnp.bfloat16)
    down_share = lax.dynamic_slice_in_dim(w_down[0], exp_index * quarter, quarter, 1)
    expert_low = jnp.dot(hidden, down_share, preferred_element_type=jnp.float32).astype(jnp.bfloat16)
    expert_out = expert_low.reshape(sources, slots_here, quarter)
    returned = lax.all_to_all(expert_out, "pool", split_axis=0, concat_axis=0, tiled=True)
    moe_share = jnp.dot(
        combine_map,
        returned.reshape(pool_count * capacity, quarter).astype(jnp.float32),
        precision=HIGHEST,
    )
    mixed_share = lax.dynamic_slice_in_dim(mixed, exp_index * quarter, quarter, 1)
    return (mixed_share + moe_share).astype(jnp.bfloat16)


def solution(mesh):
    placed = (
        P("pool", None),
        P(),
        P(),
        P("pool", None, "exp"),
        P("pool", None, "exp"),
        P("pool", None, None),
        P(),
        P(None, "exp"),
        P(None, "exp"),
        P(None, "exp"),
        P("exp", None),
        P(),
        P("pool", None),
        P("pool", None),
        P("pool", None, None),
        P("pool", None, None),
        P("pool", None, None),
    )
    return jax.shard_map(
        on_device, mesh=mesh, in_specs=placed, out_specs=P("pool", "exp"), check_vma=False
    )
```

```python
import jax
import jax.numpy as jnp
from jax import lax
from jax.experimental import pallas as pl
from jax.experimental.pallas import tpu as pltpu
from jax.sharding import PartitionSpec as P

HEAD_SIZE = 64


NEG_FILL = -1e30
EPSILON = 1e-05
SCORE_SCALE = 0.125
HIGHEST = lax.Precision.HIGHEST


def others(value, axis):
    size = lax.axis_size(axis)
    return [
        lax.ppermute(value, axis, [(i, (i + step) % size) for i in range(size)])
        for step in range(1, size)
    ]


def split_three(value):
    high = value.astype(jnp.bfloat16).astype(jnp.float32)
    rest = value - high
    middle = rest.astype(jnp.bfloat16).astype(jnp.float32)
    return high, middle, rest - middle


HEADS = 4
QUAD = 4
ROWS = HEADS * QUAD
CHUNK = 64
PARTS = 4


def attend_kernel(
    k_hbm, v_hbm, kn_hbm, vn_hbm, q_ref, cols_ref, req_ref, out_ref,
    k_ref, v_ref, kn_ref, vn_ref, qs, sc, ob, cb, sems,
):
    rows, page_len = sc.shape
    part = k_ref.shape[0] // PARTS
    copies = []
    streams = ((k_hbm, k_ref, kn_hbm, kn_ref), (v_hbm, v_ref, vn_hbm, vn_ref))
    for whole, held, new, new_held in streams:
        for c in range(PARTS):
            at = pl.ds(c * part, part)
            copies.append(
                pltpu.make_async_copy(whole.at[at], held.at[at], sems.at[len(copies)])
            )
        copies.append(pltpu.make_async_copy(new, new_held, sems.at[len(copies)]))
    for copy in copies:
        copy.start()
    requests = q_ref.shape[0]
    half = page_len // 2
    old_quads = k_ref.shape[0] // QUAD
    quads = rows // ROWS

    def head_of(shape):
        return lax.broadcasted_iota(jnp.int32, shape, 0) % HEADS

    def lane_of(shape):
        return lax.broadcasted_iota(jnp.int32, shape, 1)

    for c in range(rows // CHUNK):
        at = slice(c * CHUNK, (c + 1) * CHUNK)
        hit = cols_ref[at, 0:1] == lane_of((CHUNK, requests))
        picked = jnp.dot(
            jnp.where(hit, 1.0, 0.0).astype(jnp.bfloat16),
            q_ref[...],
            preferred_element_type=jnp.float32,
        )
        low, high = picked[:, :page_len], picked[:, page_len:]
        head = head_of((CHUNK, page_len))
        first = lane_of((CHUNK, page_len)) < half
        near = jnp.where(head == 0, low, pltpu.roll(low, half, 1))
        far = jnp.where(head == 2, pltpu.roll(high, half, 1), high)
        keep = first == (head < 2)
        qs[at, :] = jnp.where(keep, jnp.where(head < 2, near, far), 0.0).astype(jnp.bfloat16)

    quad_row = lax.broadcasted_iota(jnp.int32, (ROWS, page_len), 0) // HEADS

    def score(i, keys):
        q16 = qs[pl.ds(pl.multiple_of(i * ROWS, ROWS), ROWS), :]
        wide = lax.dot_general(
            q16,
            keys.reshape(QUAD * page_len, page_len),
            (((1,), (1,)), ((), ())),
            preferred_element_type=jnp.float32,
        )
        got = wide[:, :page_len]
        for n in range(1, QUAD):
            got = jnp.where(quad_row == n, wide[:, n * page_len : (n + 1) * page_len], got)
        sc[pl.ds(pl.multiple_of(i * ROWS, ROWS), ROWS), :] = got * SCORE_SCALE

    for c in range(PARTS):
        copies[c].wait()

        @pl.loop(c * old_quads // PARTS, (c + 1) * old_quads // PARTS, step=8)
        def _(i):
            for n in range(8):
                score(i + n, k_ref[pl.ds((i + n) * QUAD, QUAD)])

    copies[PARTS].wait()
    for i in range(old_quads, quads):
        score(i, kn_ref[(i - old_quads) * QUAD : (i - old_quads + 1) * QUAD])

    tops, sums = [], []
    ceiling = jnp.full((8, requests), NEG_FILL, jnp.float32)
    for c in range(rows // CHUNK):
        at = slice(c * CHUNK, (c + 1) * CHUNK)
        valid = lane_of((CHUNK, page_len)) < cols_ref[at, 1:2]
        masked = jnp.where(valid, sc[at, :], NEG_FILL)
        top = jnp.max(masked, axis=1, keepdims=True)
        weight = jnp.where(valid, jnp.exp(masked - top), 0.0)
        sc[at, :] = weight
        tops.append(top)
        sums.append(jnp.sum(weight, axis=1, keepdims=True))
        hit = cols_ref[at, 0:1] == lane_of((CHUNK, requests))
        spread = jnp.where(hit, top, NEG_FILL).reshape(CHUNK // 8, 8, requests)
        ceiling = jnp.maximum(ceiling, jnp.max(spread, axis=0))
    ceiling = jnp.maximum(ceiling, pltpu.roll(ceiling, HEADS, 0))

    ob[rows:, :] = jnp.zeros((ob.shape[0] - rows, ob.shape[1]), ob.dtype)
    cb[rows:, :] = jnp.zeros((cb.shape[0] - rows, cb.shape[1]), cb.dtype)
    factors = []
    for c in range(rows // CHUNK):
        at = slice(c * CHUNK, (c + 1) * CHUNK)
        hit = cols_ref[at, 0:1] == lane_of((CHUNK, requests))
        limit = jnp.broadcast_to(ceiling[None], (CHUNK // 8, 8, requests))
        own = jnp.max(
            jnp.where(hit, limit.reshape(CHUNK, requests), NEG_FILL), axis=1, keepdims=True
        )
        factor = jnp.exp(tops[c] - own)
        factors.append(factor)
        lane = lane_of((CHUNK, page_len))
        leader = jnp.where(cols_ref[at, 2:3] > 0, own, 0.0)
        pieces = split_three(jnp.where(lane < 3 * HEADS, sums[c] * factor, leader))
        turn = (lane // HEADS) % 3
        stats = jnp.where(turn == 0, pieces[0], jnp.where(turn == 1, pieces[1], pieces[2]))
        keep = (lane % HEADS == head_of((CHUNK, page_len))) & (lane < 6 * HEADS)
        cb[at, :] = jnp.where(keep, stats, 0.0).astype(jnp.bfloat16)

    step = requests // 4

    def member(c):
        owner = lax.broadcasted_iota(jnp.int32, (step, ob.shape[0]), 0) + c * step
        return jnp.where(owner == req_ref[0:1, :], 1.0, 0.0).astype(jnp.bfloat16)

    for c in range(4):
        stats = jnp.dot(member(c), cb[...], preferred_element_type=jnp.float32)
        lane = lane_of((step, page_len))
        joined = (
            stats
            + pltpu.roll(stats, page_len - HEADS, 1)
            + pltpu.roll(stats, page_len - 2 * HEADS, 1)
        )
        high, middle, rest = split_three(joined)
        middle, rest = pltpu.roll(middle, HEADS, 1), pltpu.roll(rest, 2 * HEADS, 1)
        stats = jnp.where(lane < 3 * HEADS, rest, stats)
        stats = jnp.where(lane < 2 * HEADS, middle, stats)
        stats = jnp.where(lane < HEADS, high, stats)
        out_ref[c * step : (c + 1) * step, 2 * page_len :] = stats.astype(jnp.bfloat16)

    def blend(i, values):
        p16 = sc[pl.ds(pl.multiple_of(i * ROWS, ROWS), ROWS), :]
        parts = [jnp.where(quad_row == n, p16, 0.0) for n in range(QUAD)]
        sc[pl.ds(pl.multiple_of(i * ROWS, ROWS), ROWS), :] = jnp.dot(
            jnp.concatenate(parts, axis=1).astype(jnp.bfloat16),
            values.reshape(QUAD * page_len, page_len),
            preferred_element_type=jnp.float32,
        )

    for c in range(PARTS):
        copies[c + PARTS + 1].wait()

        @pl.loop(c * old_quads // PARTS, (c + 1) * old_quads // PARTS, step=8)
        def _(i):
            for n in range(8):
                blend(i + n, v_ref[pl.ds((i + n) * QUAD, QUAD)])

    copies[2 * PARTS + 1].wait()
    for i in range(old_quads, quads):
        blend(i, vn_ref[(i - old_quads) * QUAD : (i - old_quads + 1) * QUAD])

    for c in range(rows // CHUNK):
        at = slice(c * CHUNK, (c + 1) * CHUNK)
        value = sc[at, :] * factors[c]
        turned = pltpu.roll(value, half, 1)
        head = head_of((CHUNK, page_len))
        first = lane_of((CHUNK, page_len)) < half
        low = jnp.where(first, jnp.where(head == 0, value, 0.0), jnp.where(head == 1, turned, 0.0))
        high = jnp.where(first, jnp.where(head == 2, turned, 0.0), jnp.where(head == 3, value, 0.0))
        ob[at, :page_len] = low.astype(jnp.bfloat16)
        ob[at, page_len:] = high.astype(jnp.bfloat16)
    for c in range(4):
        total = jnp.dot(member(c), ob[...], preferred_element_type=jnp.float32)
        out_ref[c * step : (c + 1) * step, : 2 * page_len] = total.astype(jnp.bfloat16)


def attend(k_cache, v_cache, key_new, value_new, all_queries, columns, owner_row):
    slots = k_cache.shape[0] + key_new.shape[0]
    page_len, width = k_cache.shape[1:]
    rows = slots * HEADS
    padded = owner_row.shape[1]
    requests = all_queries.shape[0]
    return pl.pallas_call(
        attend_kernel,
        out_shape=jax.ShapeDtypeStruct((requests, 3 * width), jnp.bfloat16),
        in_specs=[pl.BlockSpec(memory_space=pltpu.HBM)] * 4
        + [pl.BlockSpec(memory_space=pltpu.VMEM)] * 3,
        out_specs=pl.BlockSpec(memory_space=pltpu.VMEM),
        scratch_shapes=[
            pltpu.VMEM(k_cache.shape, k_cache.dtype),
            pltpu.VMEM(v_cache.shape, v_cache.dtype),
            pltpu.VMEM(key_new.shape, key_new.dtype),
            pltpu.VMEM(value_new.shape, value_new.dtype),
            pltpu.VMEM((rows, width), jnp.bfloat16),
            pltpu.VMEM((rows, page_len), jnp.float32),
            pltpu.VMEM((padded, 2 * width), jnp.bfloat16),
            pltpu.VMEM((padded, width), jnp.bfloat16),
            pltpu.SemaphoreType.DMA((2 * PARTS + 2,)),
        ],
        compiler_params=pltpu.CompilerParams(vmem_limit_bytes=59 << 20),
        cost_estimate=pl.CostEstimate(
            flops=4 * slots * ROWS * page_len * width * 4,
            bytes_accessed=4 * slots * page_len * width + (2 << 20),
            transcendentals=rows * page_len,
        ),
        name="attend",
    )(k_cache, v_cache, key_new, value_new, all_queries, columns, owner_row)


def call(kernel, outs, args, name, scratch=(), spaces=None, flops=0, limit=24 << 20):
    spaces = spaces or [pltpu.VMEM] * len(args)
    moved = sum(part.size * part.dtype.itemsize for part in list(args) + list(outs))
    return pl.pallas_call(
        kernel,
        out_shape=tuple(outs),
        in_specs=[pl.BlockSpec(memory_space=space) for space in spaces],
        out_specs=tuple(pl.BlockSpec(memory_space=pltpu.VMEM) for _ in outs),
        scratch_shapes=list(scratch),
        compiler_params=pltpu.CompilerParams(vmem_limit_bytes=limit),
        cost_estimate=pl.CostEstimate(flops=flops, bytes_accessed=moved, transcendentals=0),
        name=name,
    )(*args)


def query_kernel(tokens_ref, gain_ref, w_ref, out_ref):
    rows = rms_scale(tokens_ref[...].astype(jnp.float32), gain_ref[...].astype(jnp.float32))
    queries = jnp.dot(rows.astype(jnp.bfloat16), w_ref[...], preferred_element_type=jnp.float32)
    out_ref[...] = jnp.broadcast_to(queries.astype(jnp.bfloat16)[None], out_ref.shape)


def prepare_kernel(
    first_ref, hidden_hbm, table_ref, lengths_ref, wk_ref, wv_ref,
    kn_ref, vn_ref, cols_ref, row_ref,
    hidden_ref, turned, places, w_both, sems,
):
    part = hidden_ref.shape[0] // PARTS
    copies = []
    for c in range(PARTS):
        at = pl.ds(c * part, part)
        copies.append(pltpu.make_async_copy(hidden_hbm.at[at], hidden_ref.at[at], sems.at[c]))
    for copy in copies:
        copy.start()
    slots, requests = places.shape
    page_len = turned.shape[0]
    lanes = 128
    width = kn_ref.shape[1]
    w_both[:, :width] = wk_ref[...]
    w_both[:, width:] = wv_ref[...]
    ids = lax.broadcasted_iota(jnp.int32, (slots, lanes), 0) + first_ref[0]
    for g in range(requests // lanes):
        at = slice(g * lanes, (g + 1) * lanes)
        turned[:, at] = jnp.transpose(table_ref[at, :])
        longest = jnp.max(lengths_ref[g : g + 1, :].astype(jnp.float32)).astype(jnp.int32)

        def look(n, found, at=at):
            block = turned[pl.ds(pl.multiple_of(n * 8, 8), 8), at]
            for u in range(8):
                found = jnp.where(block[u : u + 1, :] == ids, n * 8 + u + 1, found)
            return found

        steps = (longest + 8 * page_len - 1) // (8 * page_len)
        places[:, at] = lax.fori_loop(0, steps, look, jnp.zeros((slots, lanes), jnp.int32))
    request = jnp.zeros((slots, 1), jnp.float32)
    limit = jnp.zeros((slots, 1), jnp.float32)
    leads = jnp.zeros((slots, 1), jnp.float32)
    slot = lax.broadcasted_iota(jnp.int32, (slots, lanes), 0)
    lane = lax.broadcasted_iota(jnp.int32, (slots, lanes), 1)

    def total(hit, value):
        return jnp.sum(jnp.where(hit, value.astype(jnp.float32), 0.0), axis=1, keepdims=True)

    for g in range(requests // lanes):
        place = places[:, g * lanes : (g + 1) * lanes]
        hit = place > 0
        request += total(hit, lane + g * lanes)
        limit += total(hit, lengths_ref[g : g + 1, :] - (place - 1) * page_len)
        order = jnp.where(hit, slot, slots).astype(jnp.float32)
        leads += total(hit & (order == jnp.min(order, axis=0, keepdims=True)), jnp.ones_like(lane))
    info = jnp.where(lane == 0, request, jnp.where(lane == 1, limit, leads)).astype(jnp.int32)
    rows = slots * HEADS
    cols_ref[rows:, :] = jnp.full((cols_ref.shape[0] - rows, lanes), -1, jnp.int32)
    for h in range(HEADS):
        cols_ref[pl.ds(h, slots, stride=HEADS), :] = info
    for c in range(cols_ref.shape[0] // lanes):
        at = slice(c * lanes, (c + 1) * lanes)
        row_ref[:, at] = jnp.transpose(cols_ref[at, :])[:8]
    for c in range(PARTS):
        copies[c].wait()
        at = slice(c * part, (c + 1) * part)
        both = jnp.dot(hidden_ref[at, :], w_both[...], preferred_element_type=jnp.float32)
        kn_ref[at, :] = both[:, :width].astype(jnp.bfloat16)
        vn_ref[at, :] = both[:, width:].astype(jnp.bfloat16)


def join_kernel(landed_ref, w_ref, out_ref):
    sources, owned, wide = landed_ref.shape
    lanes = wide // 3
    stats = landed_ref[:, :, 2 * lanes :].astype(jnp.float32).reshape(sources * owned, lanes)
    stats = (
        stats + pltpu.roll(stats, lanes - HEADS, 1) + pltpu.roll(stats, lanes - 2 * HEADS, 1)
    )
    lane = lax.broadcasted_iota(jnp.int32, stats.shape, 1)
    sums = jnp.where(lane < HEADS, stats, 0.0)
    tops = jnp.where(sums > 0.0, pltpu.roll(stats, lanes - 3 * HEADS, 1), NEG_FILL)
    tops = tops.reshape(sources, owned, lanes)
    weights = jnp.exp(tops - jnp.max(tops, axis=0, keepdims=True))
    totals = jnp.sum(weights * sums.reshape(sources, owned, lanes), axis=0)
    lane = lax.broadcasted_iota(jnp.int32, (1, lanes), 1)
    weights = weights.reshape(sources * owned, lanes)

    def spread(value, n):
        return jnp.where(lane < lanes // 2, value[:, 2 * n : 2 * n + 1], value[:, 2 * n + 1 : 2 * n + 2])

    projected = jnp.zeros(out_ref.shape, jnp.float32)
    for n in range(2):
        at = slice(n * lanes, (n + 1) * lanes)
        value = landed_ref[:, :, at].astype(jnp.float32).reshape(sources * owned, lanes)
        value = jnp.sum((value * spread(weights, n)).reshape(sources, owned, lanes), axis=0)
        attended = (value / spread(totals, n)).astype(jnp.bfloat16)
        projected += jnp.dot(attended, w_ref[at, :], preferred_element_type=jnp.float32)
    out_ref[...] = projected


def dispatch_kernel(tokens_ref, gain_ref, send_ref, *refs):
    *share_refs, mixed_ref, out_ref = refs
    mixed = tokens_ref[...].astype(jnp.float32) + sum(share[...] for share in share_refs)
    mixed_ref[...] = mixed
    normed = rms_scale(mixed, gain_ref[...].astype(jnp.float32)).astype(jnp.bfloat16)
    out_ref[...] = jnp.dot(send_ref[...], normed, preferred_element_type=jnp.float32).astype(
        jnp.bfloat16
    )


def rms_scale(row_vals, gain_row):
    mean_sq = jnp.mean(row_vals * row_vals, axis=-1, keepdims=True)
    return row_vals * lax.rsqrt(mean_sq + EPSILON) * gain_row


def on_device(
    tokens,
    block_table,
    lengths,
    k_cache,
    v_cache,
    hidden_store,
    norm_attn,
    w_query,
    w_key,
    w_value,
    w_out,
    norm_moe,
    expert_ids,
    gate_weights,
    w_gate,
    w_up,
    w_down,
):
    pool_count = lax.axis_size("pool")
    exp_count = lax.axis_size("exp")
    pool_index = lax.axis_index("pool")
    exp_index = lax.axis_index("exp")
    req_dev = tokens.shape[0]
    model_width = tokens.shape[1]
    quarter = model_width // exp_count
    bf16 = jnp.bfloat16
    query_width = w_query.shape[1]
    head_count = query_width // HEAD_SIZE
    (copies,) = call(
        query_kernel,
        [jax.ShapeDtypeStruct((pool_count, req_dev, query_width), bf16)],
        [tokens, norm_attn, w_query],
        "query",
        limit=60 << 20,
    )
    all_queries = lax.all_to_all(copies, "pool", split_axis=0, concat_axis=0, tiled=True)
    all_queries = all_queries.reshape(-1, query_width)
    slot_count = k_cache.shape[0] + hidden_store.shape[0]
    page_len, key_width = k_cache.shape[1:]
    requests = block_table.shape[0]
    stored_rows = hidden_store.reshape(-1, model_width)
    padded = -(-slot_count * head_count // 128) * 128
    key_new, value_new, columns, owner_row = call(
        prepare_kernel,
        [jax.ShapeDtypeStruct((stored_rows.shape[0], key_width), bf16)] * 2
        + [
            jax.ShapeDtypeStruct((padded, 128), jnp.int32),
            jax.ShapeDtypeStruct((8, padded), jnp.int32),
        ],
        [
            jnp.full((1,), pool_index * slot_count, jnp.int32),
            stored_rows,
            block_table,
            lengths.reshape(-1, 128),
            w_key,
            w_value,
        ],
        "prepare",
        [
            pltpu.VMEM(stored_rows.shape, bf16),
            pltpu.VMEM((block_table.shape[1], requests), jnp.int32),
            pltpu.VMEM((slot_count, requests), jnp.int32),
            pltpu.VMEM((model_width, 2 * key_width), bf16),
            pltpu.SemaphoreType.DMA((PARTS,)),
        ],
        [pltpu.SMEM, pltpu.HBM] + [pltpu.VMEM] * 4,
        4 * stored_rows.size * key_width,
        60 << 20,
    )
    key_new = key_new.reshape(-1, page_len, key_width)
    value_new = value_new.reshape(-1, page_len, key_width)
    parcel = attend(k_cache, v_cache, key_new, value_new, all_queries, columns, owner_row)
    parcel = parcel.reshape(pool_count, req_dev, -1)
    landed = lax.all_to_all(parcel, "pool", split_axis=0, concat_axis=0, tiled=True)
    (projected,) = call(
        join_kernel,
        [jax.ShapeDtypeStruct((req_dev, model_width), jnp.float32)],
        [landed, w_out],
        "join",
    )
    shares = [projected] + others(projected, "exp")
    top_count = expert_ids.shape[1]
    capacity = min(req_dev, 2 * ((req_dev * top_count + pool_count - 1) // pool_count))
    route_flat = expert_ids.reshape(-1)
    expert_hit = (route_flat[:, None] == jnp.arange(pool_count, dtype=jnp.int32)[None, :]).astype(
        jnp.int32
    )
    slot_rank = jnp.sum(jnp.cumsum(expert_hit, axis=0) * expert_hit, axis=1) - 1
    slot_pos = route_flat * capacity + slot_rank
    placed = (
        slot_pos[:, None] == jnp.arange(pool_count * capacity, dtype=jnp.int32)[None, :]
    ).astype(jnp.float32)
    placed = placed.reshape(req_dev, top_count, pool_count * capacity)
    send_map = jnp.sum(placed, axis=1).astype(jnp.bfloat16)
    combine_map = jnp.einsum("tk,tkc->tc", gate_weights, placed, precision=HIGHEST)
    mixed, outgoing = call(
        dispatch_kernel,
        [
            jax.ShapeDtypeStruct((req_dev, model_width), jnp.float32),
            jax.ShapeDtypeStruct((pool_count * capacity, model_width), bf16),
        ],
        [tokens, norm_moe, send_map.T] + shares,
        "dispatch",
    )
    outgoing = outgoing.reshape(pool_count, capacity, model_width)
    arrived = lax.all_to_all(outgoing, "pool", split_axis=0, concat_axis=0, tiled=True)
    sources = arrived.shape[0]
    slots_here = arrived.shape[1]
    row_block = arrived.reshape(-1, model_width)
    gate_act = jnp.dot(row_block, w_gate[0], preferred_element_type=jnp.float32)
    up_act = jnp.dot(row_block, w_up[0], preferred_element_type=jnp.float32)
    hidden = (jax.nn.silu(gate_act) * up_act).astype(jnp.bfloat16)
    down_share = lax.dynamic_slice_in_dim(w_down[0], exp_index * quarter, quarter, 1)
    expert_low = jnp.dot(hidden, down_share, preferred_element_type=jnp.float32).astype(jnp.bfloat16)
    expert_out = expert_low.reshape(sources, slots_here, quarter)
    returned = lax.all_to_all(expert_out, "pool", split_axis=0, concat_axis=0, tiled=True)
    moe_share = jnp.dot(
        combine_map,
        returned.reshape(pool_count * capacity, quarter).astype(jnp.float32),
        precision=HIGHEST,
    )
    mixed_share = lax.dynamic_slice_in_dim(mixed, exp_index * quarter, quarter, 1)
    return (mixed_share + moe_share).astype(jnp.bfloat16)


def solution(mesh):
    placed = (
        P("pool", None),
        P(),
        P(),
        P("pool", None, "exp"),
        P("pool", None, "exp"),
        P("pool", None, None),
        P(),
        P(None, "exp"),
        P(None, "exp"),
        P(None, "exp"),
        P("exp", None),
        P(),
        P("pool", None),
        P("pool", None),
        P("pool", None, None),
        P("pool", None, None),
        P("pool", None, None),
    )
    return jax.shard_map(
        on_device, mesh=mesh, in_specs=placed, out_specs=P("pool", "exp"), check_vma=False
    )
```

```python
import jax
import jax.numpy as jnp
from jax import lax
from jax.experimental import pallas as pl
from jax.experimental.pallas import tpu as pltpu
from jax.sharding import PartitionSpec as P

HEAD_SIZE = 64


NEG_FILL = -1e30
EPSILON = 1e-05
SCORE_SCALE = 0.125
HIGHEST = lax.Precision.HIGHEST


def others(value, axis):
    size = lax.axis_size(axis)
    return [
        lax.ppermute(value, axis, [(i, (i + step) % size) for i in range(size)])
        for step in range(1, size)
    ]


def split_three(value):
    high = value.astype(jnp.bfloat16).astype(jnp.float32)
    rest = value - high
    middle = rest.astype(jnp.bfloat16).astype(jnp.float32)
    return high, middle, rest - middle


HEADS = 4
QUAD = 4
ROWS = HEADS * QUAD
CHUNK = 64
PARTS = 4
SPLIT = 2
FLIGHT = 3


def attend_kernel(
    k_hbm, v_hbm, kn_hbm, vn_hbm, q_ref, cols_ref, req_ref, out_ref,
    k_ref, v_ref, kn_ref, vn_ref, qs, sc, ob, cb, sems,
):
    rows, page_len = sc.shape
    part = k_ref.shape[0] // SPLIT
    copies = []
    streams = ((k_hbm, k_ref, kn_hbm, kn_ref), (v_hbm, v_ref, vn_hbm, vn_ref))
    for whole, held, new, new_held in streams:
        for c in range(SPLIT):
            at = pl.ds(c * part, part)
            copies.append(
                pltpu.make_async_copy(whole.at[at], held.at[at], sems.at[len(copies)])
            )
        copies.append(pltpu.make_async_copy(new, new_held, sems.at[len(copies)]))
    for copy in copies[:FLIGHT]:
        copy.start()

    def arrive(n):
        copies[n].wait()
        if n + FLIGHT < len(copies):
            copies[n + FLIGHT].start()

    requests = q_ref.shape[0]
    half = page_len // 2
    old_quads = k_ref.shape[0] // QUAD
    quads = rows // ROWS

    def head_of(shape):
        return lax.broadcasted_iota(jnp.int32, shape, 0) % HEADS

    def lane_of(shape):
        return lax.broadcasted_iota(jnp.int32, shape, 1)

    for c in range(rows // CHUNK):
        at = slice(c * CHUNK, (c + 1) * CHUNK)
        hit = cols_ref[at, 0:1] == lane_of((CHUNK, requests))
        picked = jnp.dot(
            jnp.where(hit, 1.0, 0.0).astype(jnp.bfloat16),
            q_ref[...],
            preferred_element_type=jnp.float32,
        )
        low, high = picked[:, :page_len], picked[:, page_len:]
        head = head_of((CHUNK, page_len))
        first = lane_of((CHUNK, page_len)) < half
        near = jnp.where(head == 0, low, pltpu.roll(low, half, 1))
        far = jnp.where(head == 2, pltpu.roll(high, half, 1), high)
        keep = first == (head < 2)
        qs[at, :] = jnp.where(keep, jnp.where(head < 2, near, far), 0.0).astype(jnp.bfloat16)

    quad_row = lax.broadcasted_iota(jnp.int32, (ROWS, page_len), 0) // HEADS

    def score(i, keys):
        q16 = qs[i * ROWS : (i + 1) * ROWS, :]
        wide = lax.dot_general(
            q16,
            keys.reshape(QUAD * page_len, page_len),
            (((1,), (1,)), ((), ())),
            preferred_element_type=jnp.float32,
        )
        got = wide[:, :page_len]
        for n in range(1, QUAD):
            got = jnp.where(quad_row == n, wide[:, n * page_len : (n + 1) * page_len], got)
        sc[i * ROWS : (i + 1) * ROWS, :] = got * SCORE_SCALE

    for c in range(SPLIT):
        arrive(c)
        for i in range(c * old_quads // SPLIT, (c + 1) * old_quads // SPLIT):
            score(i, k_ref[i * QUAD : (i + 1) * QUAD])

    arrive(SPLIT)
    for i in range(old_quads, quads):
        score(i, kn_ref[(i - old_quads) * QUAD : (i - old_quads + 1) * QUAD])

    tops, sums = [], []
    ceiling = jnp.full((8, requests), NEG_FILL, jnp.float32)
    for c in range(rows // CHUNK):
        at = slice(c * CHUNK, (c + 1) * CHUNK)
        valid = lane_of((CHUNK, page_len)) < cols_ref[at, 1:2]
        masked = jnp.where(valid, sc[at, :], NEG_FILL)
        top = jnp.max(masked, axis=1, keepdims=True)
        weight = jnp.where(valid, jnp.exp(masked - top), 0.0)
        sc[at, :] = weight
        tops.append(top)
        sums.append(jnp.sum(weight, axis=1, keepdims=True))
        hit = cols_ref[at, 0:1] == lane_of((CHUNK, requests))
        spread = jnp.where(hit, top, NEG_FILL).reshape(CHUNK // 8, 8, requests)
        ceiling = jnp.maximum(ceiling, jnp.max(spread, axis=0))
    ceiling = jnp.maximum(ceiling, pltpu.roll(ceiling, HEADS, 0))

    ob[rows:, :] = jnp.zeros((ob.shape[0] - rows, ob.shape[1]), ob.dtype)
    cb[rows:, :] = jnp.zeros((cb.shape[0] - rows, cb.shape[1]), cb.dtype)
    factors = []
    for c in range(rows // CHUNK):
        at = slice(c * CHUNK, (c + 1) * CHUNK)
        hit = cols_ref[at, 0:1] == lane_of((CHUNK, requests))
        limit = jnp.broadcast_to(ceiling[None], (CHUNK // 8, 8, requests))
        own = jnp.max(
            jnp.where(hit, limit.reshape(CHUNK, requests), NEG_FILL), axis=1, keepdims=True
        )
        factor = jnp.exp(tops[c] - own)
        factors.append(factor)
        lane = lane_of((CHUNK, page_len))
        leader = jnp.where(cols_ref[at, 2:3] > 0, own, 0.0)
        pieces = split_three(jnp.where(lane < 3 * HEADS, sums[c] * factor, leader))
        turn = (lane // HEADS) % 3
        stats = jnp.where(turn == 0, pieces[0], jnp.where(turn == 1, pieces[1], pieces[2]))
        keep = (lane % HEADS == head_of((CHUNK, page_len))) & (lane < 6 * HEADS)
        cb[at, :] = jnp.where(keep, stats, 0.0).astype(jnp.bfloat16)

    step = requests // 4

    def member(c):
        owner = lax.broadcasted_iota(jnp.int32, (step, ob.shape[0]), 0) + c * step
        return jnp.where(owner == req_ref[0:1, :], 1.0, 0.0).astype(jnp.bfloat16)

    for c in range(4):
        stats = jnp.dot(member(c), cb[...], preferred_element_type=jnp.float32)
        lane = lane_of((step, page_len))
        joined = (
            stats
            + pltpu.roll(stats, page_len - HEADS, 1)
            + pltpu.roll(stats, page_len - 2 * HEADS, 1)
        )
        high, middle, rest = split_three(joined)
        middle, rest = pltpu.roll(middle, HEADS, 1), pltpu.roll(rest, 2 * HEADS, 1)
        stats = jnp.where(lane < 3 * HEADS, rest, stats)
        stats = jnp.where(lane < 2 * HEADS, middle, stats)
        stats = jnp.where(lane < HEADS, high, stats)
        out_ref[c * step : (c + 1) * step, 2 * page_len :] = stats.astype(jnp.bfloat16)

    def blend(i, values):
        p16 = sc[i * ROWS : (i + 1) * ROWS, :]
        parts = [jnp.where(quad_row == n, p16, 0.0) for n in range(QUAD)]
        sc[i * ROWS : (i + 1) * ROWS, :] = jnp.dot(
            jnp.concatenate(parts, axis=1).astype(jnp.bfloat16),
            values.reshape(QUAD * page_len, page_len),
            preferred_element_type=jnp.float32,
        )

    for c in range(SPLIT):
        arrive(c + SPLIT + 1)
        for i in range(c * old_quads // SPLIT, (c + 1) * old_quads // SPLIT):
            blend(i, v_ref[i * QUAD : (i + 1) * QUAD])

    arrive(2 * SPLIT + 1)
    for i in range(old_quads, quads):
        blend(i, vn_ref[(i - old_quads) * QUAD : (i - old_quads + 1) * QUAD])

    for c in range(rows // CHUNK):
        at = slice(c * CHUNK, (c + 1) * CHUNK)
        value = sc[at, :] * factors[c]
        turned = pltpu.roll(value, half, 1)
        head = head_of((CHUNK, page_len))
        first = lane_of((CHUNK, page_len)) < half
        low = jnp.where(first, jnp.where(head == 0, value, 0.0), jnp.where(head == 1, turned, 0.0))
        high = jnp.where(first, jnp.where(head == 2, turned, 0.0), jnp.where(head == 3, value, 0.0))
        ob[at, :page_len] = low.astype(jnp.bfloat16)
        ob[at, page_len:] = high.astype(jnp.bfloat16)
    for c in range(4):
        total = jnp.dot(member(c), ob[...], preferred_element_type=jnp.float32)
        out_ref[c * step : (c + 1) * step, : 2 * page_len] = total.astype(jnp.bfloat16)


def attend(k_cache, v_cache, key_new, value_new, all_queries, columns, owner_row):
    slots = k_cache.shape[0] + key_new.shape[0]
    page_len, width = k_cache.shape[1:]
    rows = slots * HEADS
    padded = owner_row.shape[1]
    requests = all_queries.shape[0]
    return pl.pallas_call(
        attend_kernel,
        out_shape=jax.ShapeDtypeStruct((requests, 3 * width), jnp.bfloat16),
        in_specs=[pl.BlockSpec(memory_space=pltpu.HBM)] * 4
        + [pl.BlockSpec(memory_space=pltpu.VMEM)] * 3,
        out_specs=pl.BlockSpec(memory_space=pltpu.VMEM),
        scratch_shapes=[
            pltpu.VMEM(k_cache.shape, k_cache.dtype),
            pltpu.VMEM(v_cache.shape, v_cache.dtype),
            pltpu.VMEM(key_new.shape, key_new.dtype),
            pltpu.VMEM(value_new.shape, value_new.dtype),
            pltpu.VMEM((rows, width), jnp.bfloat16),
            pltpu.VMEM((rows, page_len), jnp.float32),
            pltpu.VMEM((padded, 2 * width), jnp.bfloat16),
            pltpu.VMEM((padded, width), jnp.bfloat16),
            pltpu.SemaphoreType.DMA((2 * SPLIT + 2,)),
        ],
        compiler_params=pltpu.CompilerParams(vmem_limit_bytes=59 << 20),
        cost_estimate=pl.CostEstimate(
            flops=4 * slots * ROWS * page_len * width * 4,
            bytes_accessed=4 * slots * page_len * width + (2 << 20),
            transcendentals=rows * page_len,
        ),
        name="attend",
    )(k_cache, v_cache, key_new, value_new, all_queries, columns, owner_row)


def call(kernel, outs, args, name, scratch=(), spaces=None, flops=0, limit=24 << 20):
    spaces = spaces or [pltpu.VMEM] * len(args)
    moved = sum(part.size * part.dtype.itemsize for part in list(args) + list(outs))
    return pl.pallas_call(
        kernel,
        out_shape=tuple(outs),
        in_specs=[pl.BlockSpec(memory_space=space) for space in spaces],
        out_specs=tuple(pl.BlockSpec(memory_space=pltpu.VMEM) for _ in outs),
        scratch_shapes=list(scratch),
        compiler_params=pltpu.CompilerParams(vmem_limit_bytes=limit),
        cost_estimate=pl.CostEstimate(flops=flops, bytes_accessed=moved, transcendentals=0),
        name=name,
    )(*args)


def query_kernel(tokens_ref, gain_ref, w_ref, out_ref):
    rows = rms_scale(tokens_ref[...].astype(jnp.float32), gain_ref[...].astype(jnp.float32))
    queries = jnp.dot(rows.astype(jnp.bfloat16), w_ref[...], preferred_element_type=jnp.float32)
    out_ref[...] = jnp.broadcast_to(queries.astype(jnp.bfloat16)[None], out_ref.shape)


def prepare_kernel(
    first_ref, hidden_hbm, table_hbm, lengths_ref, wk_hbm, wv_hbm,
    kn_ref, vn_ref, cols_ref, row_ref,
    hidden_ref, table_ref, turned, places, w_both, sems,
):
    part = hidden_ref.shape[0] // PARTS
    width = kn_ref.shape[1]
    copies = []
    early = (
        (table_hbm, table_ref),
        (wk_hbm, w_both.at[:, pl.ds(0, width)]),
        (wv_hbm, w_both.at[:, pl.ds(width, width)]),
    )
    first_copies = []
    for n, (whole, held) in enumerate(early):
        first_copies.append(pltpu.make_async_copy(whole, held, sems.at[PARTS + n]))
    for copy in first_copies:
        copy.start()
    for c in range(PARTS):
        at = pl.ds(c * part, part)
        copies.append(pltpu.make_async_copy(hidden_hbm.at[at], hidden_ref.at[at], sems.at[c]))
    for copy in copies:
        copy.start()
    slots, requests = places.shape
    page_len = turned.shape[0]
    lanes = 128
    first_copies[0].wait()
    ids = lax.broadcasted_iota(jnp.int32, (slots, lanes), 0) + first_ref[0]
    for g in range(requests // lanes):
        at = slice(g * lanes, (g + 1) * lanes)
        turned[:, at] = jnp.transpose(table_ref[at, :])
        longest = jnp.max(lengths_ref[g : g + 1, :].astype(jnp.float32)).astype(jnp.int32)

        def look(n, found, at=at):
            block = turned[pl.ds(pl.multiple_of(n * 8, 8), 8), at]
            for u in range(8):
                found = jnp.where(block[u : u + 1, :] == ids, n * 8 + u + 1, found)
            return found

        steps = (longest + 8 * page_len - 1) // (8 * page_len)
        places[:, at] = lax.fori_loop(0, steps, look, jnp.zeros((slots, lanes), jnp.int32))
    request = jnp.zeros((slots, 1), jnp.float32)
    limit = jnp.zeros((slots, 1), jnp.float32)
    leads = jnp.zeros((slots, 1), jnp.float32)
    slot = lax.broadcasted_iota(jnp.int32, (slots, lanes), 0)
    lane = lax.broadcasted_iota(jnp.int32, (slots, lanes), 1)

    def total(hit, value):
        return jnp.sum(jnp.where(hit, value.astype(jnp.float32), 0.0), axis=1, keepdims=True)

    for g in range(requests // lanes):
        place = places[:, g * lanes : (g + 1) * lanes]
        hit = place > 0
        request += total(hit, lane + g * lanes)
        limit += total(hit, lengths_ref[g : g + 1, :] - (place - 1) * page_len)
        order = jnp.where(hit, slot, slots).astype(jnp.float32)
        leads += total(hit & (order == jnp.min(order, axis=0, keepdims=True)), jnp.ones_like(lane))
    info = jnp.where(lane == 0, request, jnp.where(lane == 1, limit, leads)).astype(jnp.int32)
    rows = slots * HEADS
    cols_ref[rows:, :] = jnp.full((cols_ref.shape[0] - rows, lanes), -1, jnp.int32)
    for h in range(HEADS):
        cols_ref[pl.ds(h, slots, stride=HEADS), :] = info
    for c in range(cols_ref.shape[0] // lanes):
        at = slice(c * lanes, (c + 1) * lanes)
        row_ref[:, at] = jnp.transpose(cols_ref[at, :])[:8]
    for copy in first_copies[1:]:
        copy.wait()
    for c in range(PARTS):
        copies[c].wait()
        at = slice(c * part, (c + 1) * part)
        both = jnp.dot(hidden_ref[at, :], w_both[...], preferred_element_type=jnp.float32)
        kn_ref[at, :] = both[:, :width].astype(jnp.bfloat16)
        vn_ref[at, :] = both[:, width:].astype(jnp.bfloat16)


def join_kernel(landed_ref, w_ref, out_ref):
    sources, owned, wide = landed_ref.shape
    lanes = wide // 3
    stats = landed_ref[:, :, 2 * lanes :].astype(jnp.float32).reshape(sources * owned, lanes)
    stats = (
        stats + pltpu.roll(stats, lanes - HEADS, 1) + pltpu.roll(stats, lanes - 2 * HEADS, 1)
    )
    lane = lax.broadcasted_iota(jnp.int32, stats.shape, 1)
    sums = jnp.where(lane < HEADS, stats, 0.0)
    tops = jnp.where(sums > 0.0, pltpu.roll(stats, lanes - 3 * HEADS, 1), NEG_FILL)
    tops = tops.reshape(sources, owned, lanes)
    weights = jnp.exp(tops - jnp.max(tops, axis=0, keepdims=True))
    totals = jnp.sum(weights * sums.reshape(sources, owned, lanes), axis=0)
    lane = lax.broadcasted_iota(jnp.int32, (1, lanes), 1)
    weights = weights.reshape(sources * owned, lanes)

    def spread(value, n):
        return jnp.where(lane < lanes // 2, value[:, 2 * n : 2 * n + 1], value[:, 2 * n + 1 : 2 * n + 2])

    projected = jnp.zeros(out_ref.shape, jnp.float32)
    for n in range(2):
        at = slice(n * lanes, (n + 1) * lanes)
        value = landed_ref[:, :, at].astype(jnp.float32).reshape(sources * owned, lanes)
        value = jnp.sum((value * spread(weights, n)).reshape(sources, owned, lanes), axis=0)
        attended = (value / spread(totals, n)).astype(jnp.bfloat16)
        projected += jnp.dot(attended, w_ref[at, :], preferred_element_type=jnp.float32)
    out_ref[...] = projected


def dispatch_kernel(tokens_ref, gain_ref, send_ref, *refs):
    *share_refs, mixed_ref, out_ref = refs
    mixed = tokens_ref[...].astype(jnp.float32) + sum(share[...] for share in share_refs)
    mixed_ref[...] = mixed
    normed = rms_scale(mixed, gain_ref[...].astype(jnp.float32)).astype(jnp.bfloat16)
    out_ref[...] = jnp.dot(send_ref[...], normed, preferred_element_type=jnp.float32).astype(
        jnp.bfloat16
    )


def expert_kernel(rows_ref, gate_ref, up_ref, down_ref, out_ref):
    rows = rows_ref[...]
    gate = jnp.dot(rows, gate_ref[...], preferred_element_type=jnp.float32)
    up = jnp.dot(rows, up_ref[...], preferred_element_type=jnp.float32)
    hidden = (gate / (1.0 + jnp.exp(-gate)) * up).astype(jnp.bfloat16)
    out_ref[...] = jnp.dot(hidden, down_ref[...], preferred_element_type=jnp.float32).astype(
        jnp.bfloat16
    )


def rms_scale(row_vals, gain_row):
    mean_sq = jnp.mean(row_vals * row_vals, axis=-1, keepdims=True)
    return row_vals * lax.rsqrt(mean_sq + EPSILON) * gain_row


def on_device(
    tokens,
    block_table,
    lengths,
    k_cache,
    v_cache,
    hidden_store,
    norm_attn,
    w_query,
    w_key,
    w_value,
    w_out,
    norm_moe,
    expert_ids,
    gate_weights,
    w_gate,
    w_up,
    w_down,
):
    pool_count = lax.axis_size("pool")
    exp_count = lax.axis_size("exp")
    pool_index = lax.axis_index("pool")
    exp_index = lax.axis_index("exp")
    req_dev = tokens.shape[0]
    model_width = tokens.shape[1]
    quarter = model_width // exp_count
    bf16 = jnp.bfloat16
    query_width = w_query.shape[1]
    head_count = query_width // HEAD_SIZE
    (copies,) = call(
        query_kernel,
        [jax.ShapeDtypeStruct((pool_count, req_dev, query_width), bf16)],
        [tokens, norm_attn, w_query],
        "query",
        limit=60 << 20,
    )
    all_queries = lax.all_to_all(copies, "pool", split_axis=0, concat_axis=0, tiled=True)
    all_queries = all_queries.reshape(-1, query_width)
    slot_count = k_cache.shape[0] + hidden_store.shape[0]
    page_len, key_width = k_cache.shape[1:]
    requests = block_table.shape[0]
    stored_rows = hidden_store.reshape(-1, model_width)
    padded = -(-slot_count * head_count // 128) * 128
    key_new, value_new, columns, owner_row = call(
        prepare_kernel,
        [jax.ShapeDtypeStruct((stored_rows.shape[0], key_width), bf16)] * 2
        + [
            jax.ShapeDtypeStruct((padded, 128), jnp.int32),
            jax.ShapeDtypeStruct((8, padded), jnp.int32),
        ],
        [
            jnp.full((1,), pool_index * slot_count, jnp.int32),
            stored_rows,
            block_table,
            lengths.reshape(-1, 128),
            w_key,
            w_value,
        ],
        "prepare",
        [
            pltpu.VMEM(stored_rows.shape, bf16),
            pltpu.VMEM(block_table.shape, jnp.int32),
            pltpu.VMEM((block_table.shape[1], requests), jnp.int32),
            pltpu.VMEM((slot_count, requests), jnp.int32),
            pltpu.VMEM((model_width, 2 * key_width), bf16),
            pltpu.SemaphoreType.DMA((PARTS + 3,)),
        ],
        [pltpu.SMEM, pltpu.HBM, pltpu.HBM, pltpu.VMEM, pltpu.HBM, pltpu.HBM],
        4 * stored_rows.size * key_width,
        60 << 20,
    )
    key_new = key_new.reshape(-1, page_len, key_width)
    value_new = value_new.reshape(-1, page_len, key_width)
    parcel = attend(k_cache, v_cache, key_new, value_new, all_queries, columns, owner_row)
    parcel, expert_ids, w_down = lax.optimization_barrier((parcel, expert_ids, w_down))
    down_share = lax.dynamic_slice_in_dim(w_down[0], exp_index * quarter, quarter, 1)
    parcel = parcel.reshape(pool_count, req_dev, -1)
    landed = lax.all_to_all(parcel, "pool", split_axis=0, concat_axis=0, tiled=True)
    (projected,) = call(
        join_kernel,
        [jax.ShapeDtypeStruct((req_dev, model_width), jnp.float32)],
        [landed, w_out],
        "join",
    )
    shares = [projected] + others(projected, "exp")
    top_count = expert_ids.shape[1]
    capacity = min(req_dev, 2 * ((req_dev * top_count + pool_count - 1) // pool_count))
    route_flat = expert_ids.reshape(-1)
    expert_hit = (route_flat[:, None] == jnp.arange(pool_count, dtype=jnp.int32)[None, :]).astype(
        jnp.int32
    )
    slot_rank = jnp.sum(jnp.cumsum(expert_hit, axis=0) * expert_hit, axis=1) - 1
    slot_pos = route_flat * capacity + slot_rank
    placed = (
        slot_pos[:, None] == jnp.arange(pool_count * capacity, dtype=jnp.int32)[None, :]
    ).astype(jnp.float32)
    placed = placed.reshape(req_dev, top_count, pool_count * capacity)
    send_map = jnp.sum(placed, axis=1).astype(jnp.bfloat16)
    combine_map = jnp.einsum("tk,tkc->tc", gate_weights, placed, precision=HIGHEST)
    mixed, outgoing = call(
        dispatch_kernel,
        [
            jax.ShapeDtypeStruct((req_dev, model_width), jnp.float32),
            jax.ShapeDtypeStruct((pool_count * capacity, model_width), bf16),
        ],
        [tokens, norm_moe, send_map.T] + shares,
        "dispatch",
    )
    outgoing = outgoing.reshape(pool_count, capacity, model_width)
    arrived = lax.all_to_all(outgoing, "pool", split_axis=0, concat_axis=0, tiled=True)
    sources = arrived.shape[0]
    slots_here = arrived.shape[1]
    row_block = arrived.reshape(-1, model_width)
    (expert_low,) = call(
        expert_kernel,
        [jax.ShapeDtypeStruct((row_block.shape[0], quarter), bf16)],
        [row_block, w_gate[0], w_up[0], down_share],
        "expert",
        flops=4 * row_block.size * w_up.shape[2],
        limit=16 << 20,
    )
    expert_out = expert_low.reshape(sources, slots_here, quarter)
    returned = lax.all_to_all(expert_out, "pool", split_axis=0, concat_axis=0, tiled=True)
    moe_share = jnp.dot(
        combine_map,
        returned.reshape(pool_count * capacity, quarter).astype(jnp.float32),
        precision=HIGHEST,
    )
    mixed_share = lax.dynamic_slice_in_dim(mixed, exp_index * quarter, quarter, 1)
    return (mixed_share + moe_share).astype(jnp.bfloat16)


def solution(mesh):
    placed = (
        P("pool", None),
        P(),
        P(),
        P("pool", None, "exp"),
        P("pool", None, "exp"),
        P("pool", None, None),
        P(),
        P(None, "exp"),
        P(None, "exp"),
        P(None, "exp"),
        P("exp", None),
        P(),
        P("pool", None),
        P("pool", None),
        P("pool", None, None),
        P("pool", None, None),
        P("pool", None, None),
    )
    return jax.shard_map(
        on_device, mesh=mesh, in_specs=placed, out_specs=P("pool", "exp"), check_vma=False
    )
```

```python
import jax
import jax.numpy as jnp
from jax import lax
from jax.experimental import pallas as pl
from jax.experimental.pallas import tpu as pltpu
from jax.sharding import PartitionSpec as P

HEAD_SIZE = 64


NEG_FILL = -1e30
EPSILON = 1e-05
SCORE_SCALE = 0.125
HIGHEST = lax.Precision.HIGHEST


def others(value, axis):
    size = lax.axis_size(axis)
    return [
        lax.ppermute(value, axis, [(i, (i + step) % size) for i in range(size)])
        for step in range(1, size)
    ]


def split_three(value):
    high = value.astype(jnp.bfloat16).astype(jnp.float32)
    rest = value - high
    middle = rest.astype(jnp.bfloat16).astype(jnp.float32)
    return high, middle, rest - middle


HEADS = 4
QUAD = 4
ROWS = HEADS * QUAD
CHUNK = 64
PARTS = 4
SPLIT = 2
FLIGHT = 6


def attend_kernel(
    k_hbm, v_hbm, kn_hbm, vn_hbm, q_ref, cols_ref, req_ref, out_ref,
    k_ref, v_ref, kn_ref, vn_ref, qs, sc, ob, cb, sems,
):
    rows, page_len = sc.shape
    part = k_ref.shape[0] // SPLIT
    copies = []
    streams = ((k_hbm, k_ref, kn_hbm, kn_ref), (v_hbm, v_ref, vn_hbm, vn_ref))
    for whole, held, new, new_held in streams:
        for c in range(SPLIT):
            at = pl.ds(c * part, part)
            copies.append(
                pltpu.make_async_copy(whole.at[at], held.at[at], sems.at[len(copies)])
            )
        copies.append(pltpu.make_async_copy(new, new_held, sems.at[len(copies)]))
    for copy in copies[:FLIGHT]:
        copy.start()

    def arrive(n):
        copies[n].wait()
        if n + FLIGHT < len(copies):
            copies[n + FLIGHT].start()

    requests = q_ref.shape[0]
    half = page_len // 2
    old_quads = k_ref.shape[0] // QUAD
    quads = rows // ROWS

    def head_of(shape):
        return lax.broadcasted_iota(jnp.int32, shape, 0) % HEADS

    def lane_of(shape):
        return lax.broadcasted_iota(jnp.int32, shape, 1)

    for c in range(rows // CHUNK):
        at = slice(c * CHUNK, (c + 1) * CHUNK)
        hit = cols_ref[at, 0:1] == lane_of((CHUNK, requests))
        picked = jnp.dot(
            jnp.where(hit, 1.0, 0.0).astype(jnp.bfloat16),
            q_ref[...],
            preferred_element_type=jnp.float32,
        )
        low, high = picked[:, :page_len], picked[:, page_len:]
        head = head_of((CHUNK, page_len))
        first = lane_of((CHUNK, page_len)) < half
        near = jnp.where(head == 0, low, pltpu.roll(low, half, 1))
        far = jnp.where(head == 2, pltpu.roll(high, half, 1), high)
        keep = first == (head < 2)
        qs[at, :] = jnp.where(keep, jnp.where(head < 2, near, far), 0.0).astype(jnp.bfloat16)

    quad_row = lax.broadcasted_iota(jnp.int32, (ROWS, page_len), 0) // HEADS

    def score(i, keys):
        q16 = qs[i * ROWS : (i + 1) * ROWS, :]
        wide = lax.dot_general(
            q16,
            keys.reshape(QUAD * page_len, page_len),
            (((1,), (1,)), ((), ())),
            preferred_element_type=jnp.float32,
        )
        got = wide[:, :page_len]
        for n in range(1, QUAD):
            got = jnp.where(quad_row == n, wide[:, n * page_len : (n + 1) * page_len], got)
        sc[i * ROWS : (i + 1) * ROWS, :] = got * SCORE_SCALE

    for c in range(SPLIT):
        arrive(c)
        for i in range(c * old_quads // SPLIT, (c + 1) * old_quads // SPLIT):
            score(i, k_ref[i * QUAD : (i + 1) * QUAD])

    arrive(SPLIT)
    for i in range(old_quads, quads):
        score(i, kn_ref[(i - old_quads) * QUAD : (i - old_quads + 1) * QUAD])

    tops, sums = [], []
    ceiling = jnp.full((8, requests), NEG_FILL, jnp.float32)
    for c in range(rows // CHUNK):
        at = slice(c * CHUNK, (c + 1) * CHUNK)
        valid = lane_of((CHUNK, page_len)) < cols_ref[at, 1:2]
        masked = jnp.where(valid, sc[at, :], NEG_FILL)
        top = jnp.max(masked, axis=1, keepdims=True)
        weight = jnp.where(valid, jnp.exp(masked - top), 0.0)
        sc[at, :] = weight
        tops.append(top)
        sums.append(jnp.sum(weight, axis=1, keepdims=True))
        hit = cols_ref[at, 0:1] == lane_of((CHUNK, requests))
        spread = jnp.where(hit, top, NEG_FILL).reshape(CHUNK // 8, 8, requests)
        ceiling = jnp.maximum(ceiling, jnp.max(spread, axis=0))
    ceiling = jnp.maximum(ceiling, pltpu.roll(ceiling, HEADS, 0))

    ob[rows:, :] = jnp.zeros((ob.shape[0] - rows, ob.shape[1]), ob.dtype)
    cb[rows:, :] = jnp.zeros((cb.shape[0] - rows, cb.shape[1]), cb.dtype)
    factors = []
    for c in range(rows // CHUNK):
        at = slice(c * CHUNK, (c + 1) * CHUNK)
        hit = cols_ref[at, 0:1] == lane_of((CHUNK, requests))
        limit = jnp.broadcast_to(ceiling[None], (CHUNK // 8, 8, requests))
        own = jnp.max(
            jnp.where(hit, limit.reshape(CHUNK, requests), NEG_FILL), axis=1, keepdims=True
        )
        factor = jnp.exp(tops[c] - own)
        factors.append(factor)
        lane = lane_of((CHUNK, page_len))
        leader = jnp.where(cols_ref[at, 2:3] > 0, own, 0.0)
        pieces = split_three(jnp.where(lane < 3 * HEADS, sums[c] * factor, leader))
        turn = (lane // HEADS) % 3
        stats = jnp.where(turn == 0, pieces[0], jnp.where(turn == 1, pieces[1], pieces[2]))
        keep = (lane % HEADS == head_of((CHUNK, page_len))) & (lane < 6 * HEADS)
        cb[at, :] = jnp.where(keep, stats, 0.0).astype(jnp.bfloat16)

    step = requests // 4

    def member(c):
        owner = lax.broadcasted_iota(jnp.int32, (step, ob.shape[0]), 0) + c * step
        return jnp.where(owner == req_ref[0:1, :], 1.0, 0.0).astype(jnp.bfloat16)

    for c in range(4):
        stats = jnp.dot(member(c), cb[...], preferred_element_type=jnp.float32)
        lane = lane_of((step, page_len))
        joined = (
            stats
            + pltpu.roll(stats, page_len - HEADS, 1)
            + pltpu.roll(stats, page_len - 2 * HEADS, 1)
        )
        high, middle, rest = split_three(joined)
        middle, rest = pltpu.roll(middle, HEADS, 1), pltpu.roll(rest, 2 * HEADS, 1)
        stats = jnp.where(lane < 3 * HEADS, rest, stats)
        stats = jnp.where(lane < 2 * HEADS, middle, stats)
        stats = jnp.where(lane < HEADS, high, stats)
        out_ref[c * step : (c + 1) * step, 2 * page_len :] = stats.astype(jnp.bfloat16)

    def blend(i, values):
        p16 = sc[i * ROWS : (i + 1) * ROWS, :]
        parts = [jnp.where(quad_row == n, p16, 0.0) for n in range(QUAD)]
        sc[i * ROWS : (i + 1) * ROWS, :] = jnp.dot(
            jnp.concatenate(parts, axis=1).astype(jnp.bfloat16),
            values.reshape(QUAD * page_len, page_len),
            preferred_element_type=jnp.float32,
        )

    for c in range(SPLIT):
        arrive(c + SPLIT + 1)
        for i in range(c * old_quads // SPLIT, (c + 1) * old_quads // SPLIT):
            blend(i, v_ref[i * QUAD : (i + 1) * QUAD])

    arrive(2 * SPLIT + 1)
    for i in range(old_quads, quads):
        blend(i, vn_ref[(i - old_quads) * QUAD : (i - old_quads + 1) * QUAD])

    for c in range(rows // CHUNK):
        at = slice(c * CHUNK, (c + 1) * CHUNK)
        value = sc[at, :] * factors[c]
        turned = pltpu.roll(value, half, 1)
        head = head_of((CHUNK, page_len))
        first = lane_of((CHUNK, page_len)) < half
        low = jnp.where(first, jnp.where(head == 0, value, 0.0), jnp.where(head == 1, turned, 0.0))
        high = jnp.where(first, jnp.where(head == 2, turned, 0.0), jnp.where(head == 3, value, 0.0))
        ob[at, :page_len] = low.astype(jnp.bfloat16)
        ob[at, page_len:] = high.astype(jnp.bfloat16)
    for c in range(4):
        total = jnp.dot(member(c), ob[...], preferred_element_type=jnp.float32)
        out_ref[c * step : (c + 1) * step, : 2 * page_len] = total.astype(jnp.bfloat16)


def attend(k_cache, v_cache, key_new, value_new, all_queries, columns, owner_row):
    slots = k_cache.shape[0] + key_new.shape[0]
    page_len, width = k_cache.shape[1:]
    rows = slots * HEADS
    padded = owner_row.shape[1]
    requests = all_queries.shape[0]
    return pl.pallas_call(
        attend_kernel,
        out_shape=jax.ShapeDtypeStruct((requests, 3 * width), jnp.bfloat16),
        in_specs=[pl.BlockSpec(memory_space=pltpu.HBM)] * 4
        + [pl.BlockSpec(memory_space=pltpu.VMEM)] * 3,
        out_specs=pl.BlockSpec(memory_space=pltpu.VMEM),
        scratch_shapes=[
            pltpu.VMEM(k_cache.shape, k_cache.dtype),
            pltpu.VMEM(v_cache.shape, v_cache.dtype),
            pltpu.VMEM(key_new.shape, key_new.dtype),
            pltpu.VMEM(value_new.shape, value_new.dtype),
            pltpu.VMEM((rows, width), jnp.bfloat16),
            pltpu.VMEM((rows, page_len), jnp.float32),
            pltpu.VMEM((padded, 2 * width), jnp.bfloat16),
            pltpu.VMEM((padded, width), jnp.bfloat16),
            pltpu.SemaphoreType.DMA((2 * SPLIT + 2,)),
        ],
        compiler_params=pltpu.CompilerParams(vmem_limit_bytes=59 << 20),
        cost_estimate=pl.CostEstimate(
            flops=4 * slots * ROWS * page_len * width * 4,
            bytes_accessed=4 * slots * page_len * width + (2 << 20),
            transcendentals=rows * page_len,
        ),
        name="attend",
    )(k_cache, v_cache, key_new, value_new, all_queries, columns, owner_row)


def call(kernel, outs, args, name, scratch=(), spaces=None, flops=0, limit=24 << 20):
    spaces = spaces or [pltpu.VMEM] * len(args)
    moved = sum(part.size * part.dtype.itemsize for part in list(args) + list(outs))
    return pl.pallas_call(
        kernel,
        out_shape=tuple(outs),
        in_specs=[pl.BlockSpec(memory_space=space) for space in spaces],
        out_specs=tuple(pl.BlockSpec(memory_space=pltpu.VMEM) for _ in outs),
        scratch_shapes=list(scratch),
        compiler_params=pltpu.CompilerParams(vmem_limit_bytes=limit),
        cost_estimate=pl.CostEstimate(flops=flops, bytes_accessed=moved, transcendentals=0),
        name=name,
    )(*args)


def query_kernel(tokens_ref, gain_ref, w_ref, out_ref):
    rows = rms_scale(tokens_ref[...].astype(jnp.float32), gain_ref[...].astype(jnp.float32))
    queries = jnp.dot(rows.astype(jnp.bfloat16), w_ref[...], preferred_element_type=jnp.float32)
    out_ref[...] = jnp.broadcast_to(queries.astype(jnp.bfloat16)[None], out_ref.shape)


def prepare_kernel(
    first_ref, hidden_hbm, table_hbm, lengths_ref, wk_hbm, wv_hbm,
    kn_ref, vn_ref, cols_ref, row_ref,
    hidden_ref, table_ref, turned, places, w_both, sems,
):
    part = hidden_ref.shape[0] // PARTS
    width = kn_ref.shape[1]
    copies = []
    early = (
        (table_hbm, table_ref),
        (wk_hbm, w_both.at[:, pl.ds(0, width)]),
        (wv_hbm, w_both.at[:, pl.ds(width, width)]),
    )
    first_copies = []
    for n, (whole, held) in enumerate(early):
        first_copies.append(pltpu.make_async_copy(whole, held, sems.at[PARTS + n]))
    for copy in first_copies:
        copy.start()
    for c in range(PARTS):
        at = pl.ds(c * part, part)
        copies.append(pltpu.make_async_copy(hidden_hbm.at[at], hidden_ref.at[at], sems.at[c]))
    for copy in copies:
        copy.start()
    slots, requests = places.shape
    page_len = turned.shape[0]
    lanes = 128
    first_copies[0].wait()
    ids = lax.broadcasted_iota(jnp.int32, (slots, lanes), 0) + first_ref[0]
    for g in range(requests // lanes):
        at = slice(g * lanes, (g + 1) * lanes)
        turned[:, at] = jnp.transpose(table_ref[at, :])
        longest = jnp.max(lengths_ref[g : g + 1, :].astype(jnp.float32)).astype(jnp.int32)

        def look(n, found, at=at):
            block = turned[pl.ds(pl.multiple_of(n * 8, 8), 8), at]
            for u in range(8):
                found = jnp.where(block[u : u + 1, :] == ids, n * 8 + u + 1, found)
            return found

        steps = (longest + 8 * page_len - 1) // (8 * page_len)
        places[:, at] = lax.fori_loop(0, steps, look, jnp.zeros((slots, lanes), jnp.int32))
    request = jnp.zeros((slots, 1), jnp.float32)
    limit = jnp.zeros((slots, 1), jnp.float32)
    leads = jnp.zeros((slots, 1), jnp.float32)
    slot = lax.broadcasted_iota(jnp.int32, (slots, lanes), 0)
    lane = lax.broadcasted_iota(jnp.int32, (slots, lanes), 1)

    def total(hit, value):
        return jnp.sum(jnp.where(hit, value.astype(jnp.float32), 0.0), axis=1, keepdims=True)

    for g in range(requests // lanes):
        place = places[:, g * lanes : (g + 1) * lanes]
        hit = place > 0
        request += total(hit, lane + g * lanes)
        limit += total(hit, lengths_ref[g : g + 1, :] - (place - 1) * page_len)
        order = jnp.where(hit, slot, slots).astype(jnp.float32)
        leads += total(hit & (order == jnp.min(order, axis=0, keepdims=True)), jnp.ones_like(lane))
    info = jnp.where(lane == 0, request, jnp.where(lane == 1, limit, leads)).astype(jnp.int32)
    rows = slots * HEADS
    cols_ref[rows:, :] = jnp.full((cols_ref.shape[0] - rows, lanes), -1, jnp.int32)
    for h in range(HEADS):
        cols_ref[pl.ds(h, slots, stride=HEADS), :] = info
    for c in range(cols_ref.shape[0] // lanes):
        at = slice(c * lanes, (c + 1) * lanes)
        row_ref[:, at] = jnp.transpose(cols_ref[at, :])[:8]
    for copy in first_copies[1:]:
        copy.wait()
    for c in range(PARTS):
        copies[c].wait()
        at = slice(c * part, (c + 1) * part)
        both = jnp.dot(hidden_ref[at, :], w_both[...], preferred_element_type=jnp.float32)
        kn_ref[at, :] = both[:, :width].astype(jnp.bfloat16)
        vn_ref[at, :] = both[:, width:].astype(jnp.bfloat16)


def join_kernel(landed_ref, w_ref, out_ref):
    sources, owned, wide = landed_ref.shape
    lanes = wide // 3
    stats = landed_ref[:, :, 2 * lanes :].astype(jnp.float32).reshape(sources * owned, lanes)
    stats = (
        stats + pltpu.roll(stats, lanes - HEADS, 1) + pltpu.roll(stats, lanes - 2 * HEADS, 1)
    )
    lane = lax.broadcasted_iota(jnp.int32, stats.shape, 1)
    sums = jnp.where(lane < HEADS, stats, 0.0)
    tops = jnp.where(sums > 0.0, pltpu.roll(stats, lanes - 3 * HEADS, 1), NEG_FILL)
    tops = tops.reshape(sources, owned, lanes)
    weights = jnp.exp(tops - jnp.max(tops, axis=0, keepdims=True))
    totals = jnp.sum(weights * sums.reshape(sources, owned, lanes), axis=0)
    lane = lax.broadcasted_iota(jnp.int32, (1, lanes), 1)
    weights = weights.reshape(sources * owned, lanes)

    def spread(value, n):
        return jnp.where(lane < lanes // 2, value[:, 2 * n : 2 * n + 1], value[:, 2 * n + 1 : 2 * n + 2])

    projected = jnp.zeros(out_ref.shape, jnp.float32)
    for n in range(2):
        at = slice(n * lanes, (n + 1) * lanes)
        value = landed_ref[:, :, at].astype(jnp.float32).reshape(sources * owned, lanes)
        value = jnp.sum((value * spread(weights, n)).reshape(sources, owned, lanes), axis=0)
        attended = (value / spread(totals, n)).astype(jnp.bfloat16)
        projected += jnp.dot(attended, w_ref[at, :], preferred_element_type=jnp.float32)
    out_ref[...] = projected


def dispatch_kernel(tokens_ref, gain_ref, send_ref, *refs):
    *share_refs, mixed_ref, out_ref = refs
    mixed = tokens_ref[...].astype(jnp.float32) + sum(share[...] for share in share_refs)
    mixed_ref[...] = mixed
    normed = rms_scale(mixed, gain_ref[...].astype(jnp.float32)).astype(jnp.bfloat16)
    out_ref[...] = jnp.dot(send_ref[...], normed, preferred_element_type=jnp.float32).astype(
        jnp.bfloat16
    )


def expert_kernel(rows_ref, gate_ref, up_ref, down_ref, out_ref):
    rows = rows_ref[...]
    gate = jnp.dot(rows, gate_ref[...], preferred_element_type=jnp.float32)
    up = jnp.dot(rows, up_ref[...], preferred_element_type=jnp.float32)
    hidden = (gate / (1.0 + jnp.exp(-gate)) * up).astype(jnp.bfloat16)
    out_ref[...] = jnp.dot(hidden, down_ref[...], preferred_element_type=jnp.float32).astype(
        jnp.bfloat16
    )


def rms_scale(row_vals, gain_row):
    mean_sq = jnp.mean(row_vals * row_vals, axis=-1, keepdims=True)
    return row_vals * lax.rsqrt(mean_sq + EPSILON) * gain_row


def on_device(
    tokens,
    block_table,
    lengths,
    k_cache,
    v_cache,
    hidden_store,
    norm_attn,
    w_query,
    w_key,
    w_value,
    w_out,
    norm_moe,
    expert_ids,
    gate_weights,
    w_gate,
    w_up,
    w_down,
):
    pool_count = lax.axis_size("pool")
    exp_count = lax.axis_size("exp")
    pool_index = lax.axis_index("pool")
    exp_index = lax.axis_index("exp")
    req_dev = tokens.shape[0]
    model_width = tokens.shape[1]
    quarter = model_width // exp_count
    bf16 = jnp.bfloat16
    query_width = w_query.shape[1]
    head_count = query_width // HEAD_SIZE
    (copies,) = call(
        query_kernel,
        [jax.ShapeDtypeStruct((pool_count, req_dev, query_width), bf16)],
        [tokens, norm_attn, w_query],
        "query",
        limit=60 << 20,
    )
    all_queries = lax.all_to_all(copies, "pool", split_axis=0, concat_axis=0, tiled=True)
    all_queries = all_queries.reshape(-1, query_width)
    slot_count = k_cache.shape[0] + hidden_store.shape[0]
    page_len, key_width = k_cache.shape[1:]
    requests = block_table.shape[0]
    stored_rows = hidden_store.reshape(-1, model_width)
    padded = -(-slot_count * head_count // 128) * 128
    key_new, value_new, columns, owner_row = call(
        prepare_kernel,
        [jax.ShapeDtypeStruct((stored_rows.shape[0], key_width), bf16)] * 2
        + [
            jax.ShapeDtypeStruct((padded, 128), jnp.int32),
            jax.ShapeDtypeStruct((8, padded), jnp.int32),
        ],
        [
            jnp.full((1,), pool_index * slot_count, jnp.int32),
            stored_rows,
            block_table,
            lengths.reshape(-1, 128),
            w_key,
            w_value,
        ],
        "prepare",
        [
            pltpu.VMEM(stored_rows.shape, bf16),
            pltpu.VMEM(block_table.shape, jnp.int32),
            pltpu.VMEM((block_table.shape[1], requests), jnp.int32),
            pltpu.VMEM((slot_count, requests), jnp.int32),
            pltpu.VMEM((model_width, 2 * key_width), bf16),
            pltpu.SemaphoreType.DMA((PARTS + 3,)),
        ],
        [pltpu.SMEM, pltpu.HBM, pltpu.HBM, pltpu.VMEM, pltpu.HBM, pltpu.HBM],
        4 * stored_rows.size * key_width,
        60 << 20,
    )
    key_new = key_new.reshape(-1, page_len, key_width)
    value_new = value_new.reshape(-1, page_len, key_width)
    parcel = attend(k_cache, v_cache, key_new, value_new, all_queries, columns, owner_row)
    parcel, w_down = lax.optimization_barrier((parcel, w_down))
    down_share = lax.dynamic_slice_in_dim(w_down[0], exp_index * quarter, quarter, 1)
    parcel = parcel.reshape(pool_count, req_dev, -1)
    landed = lax.all_to_all(parcel, "pool", split_axis=0, concat_axis=0, tiled=True)
    (projected,) = call(
        join_kernel,
        [jax.ShapeDtypeStruct((req_dev, model_width), jnp.float32)],
        [landed, w_out],
        "join",
    )
    projected, expert_ids = lax.optimization_barrier((projected, expert_ids))
    shares = [projected] + others(projected, "exp")
    top_count = expert_ids.shape[1]
    capacity = min(req_dev, 2 * ((req_dev * top_count + pool_count - 1) // pool_count))
    route_flat = expert_ids.reshape(-1)
    expert_hit = (route_flat[:, None] == jnp.arange(pool_count, dtype=jnp.int32)[None, :]).astype(
        jnp.int32
    )
    slot_rank = jnp.sum(jnp.cumsum(expert_hit, axis=0) * expert_hit, axis=1) - 1
    slot_pos = route_flat * capacity + slot_rank
    placed = (
        slot_pos[:, None] == jnp.arange(pool_count * capacity, dtype=jnp.int32)[None, :]
    ).astype(jnp.float32)
    placed = placed.reshape(req_dev, top_count, pool_count * capacity)
    send_map = jnp.sum(placed, axis=1).astype(jnp.bfloat16)
    combine_map = jnp.einsum("tk,tkc->tc", gate_weights, placed, precision=HIGHEST)
    mixed, outgoing = call(
        dispatch_kernel,
        [
            jax.ShapeDtypeStruct((req_dev, model_width), jnp.float32),
            jax.ShapeDtypeStruct((pool_count * capacity, model_width), bf16),
        ],
        [tokens, norm_moe, send_map.T] + shares,
        "dispatch",
    )
    outgoing = outgoing.reshape(pool_count, capacity, model_width)
    arrived = lax.all_to_all(outgoing, "pool", split_axis=0, concat_axis=0, tiled=True)
    sources = arrived.shape[0]
    slots_here = arrived.shape[1]
    row_block = arrived.reshape(-1, model_width)
    (expert_low,) = call(
        expert_kernel,
        [jax.ShapeDtypeStruct((row_block.shape[0], quarter), bf16)],
        [row_block, w_gate[0], w_up[0], down_share],
        "expert",
        flops=4 * row_block.size * w_up.shape[2],
        limit=16 << 20,
    )
    expert_out = expert_low.reshape(sources, slots_here, quarter)
    returned = lax.all_to_all(expert_out, "pool", split_axis=0, concat_axis=0, tiled=True)
    moe_share = jnp.dot(
        combine_map,
        returned.reshape(pool_count * capacity, quarter).astype(jnp.float32),
        precision=HIGHEST,
    )
    mixed_share = lax.dynamic_slice_in_dim(mixed, exp_index * quarter, quarter, 1)
    return (mixed_share + moe_share).astype(jnp.bfloat16)


def solution(mesh):
    placed = (
        P("pool", None),
        P(),
        P(),
        P("pool", None, "exp"),
        P("pool", None, "exp"),
        P("pool", None, None),
        P(),
        P(None, "exp"),
        P(None, "exp"),
        P(None, "exp"),
        P("exp", None),
        P(),
        P("pool", None),
        P("pool", None),
        P("pool", None, None),
        P("pool", None, None),
        P("pool", None, None),
    )
    return jax.shard_map(
        on_device, mesh=mesh, in_specs=placed, out_specs=P("pool", "exp"), check_vma=False
    )
```

```python
import jax
import jax.numpy as jnp
from jax import lax
from jax.experimental import pallas as pl
from jax.experimental.pallas import tpu as pltpu
from jax.sharding import PartitionSpec as P

HEAD_SIZE = 64


NEG_FILL = -1e30
EPSILON = 1e-05
SCORE_SCALE = 0.125
HIGHEST = lax.Precision.HIGHEST


def others(value, axis):
    size = lax.axis_size(axis)
    return [
        lax.ppermute(value, axis, [(i, (i + step) % size) for i in range(size)])
        for step in range(1, size)
    ]


def split_three(value):
    high = value.astype(jnp.bfloat16).astype(jnp.float32)
    rest = value - high
    middle = rest.astype(jnp.bfloat16).astype(jnp.float32)
    return high, middle, rest - middle


HEADS = 4
QUAD = 4
ROWS = HEADS * QUAD
CHUNK = 64
PARTS = 4
SPLIT = 2
FLIGHT = 6


def attend_kernel(
    k_hbm, v_hbm, kn_hbm, vn_hbm, q_ref, cols_ref, req_ref, out_ref,
    k_ref, v_ref, kn_ref, vn_ref, qs, sc, ob, cb, sems,
):
    rows, page_len = sc.shape
    part = k_ref.shape[0] // SPLIT
    copies = []
    streams = ((k_hbm, k_ref, kn_hbm, kn_ref), (v_hbm, v_ref, vn_hbm, vn_ref))
    for whole, held, new, new_held in streams:
        for c in range(SPLIT):
            at = pl.ds(c * part, part)
            copies.append(
                pltpu.make_async_copy(whole.at[at], held.at[at], sems.at[len(copies)])
            )
        copies.append(pltpu.make_async_copy(new, new_held, sems.at[len(copies)]))
    for copy in copies[:FLIGHT]:
        copy.start()

    def arrive(n):
        copies[n].wait()
        if n + FLIGHT < len(copies):
            copies[n + FLIGHT].start()

    requests = q_ref.shape[0]
    half = page_len // 2
    old_quads = k_ref.shape[0] // QUAD
    quads = rows // ROWS

    def head_of(shape):
        return lax.broadcasted_iota(jnp.int32, shape, 0) % HEADS

    def lane_of(shape):
        return lax.broadcasted_iota(jnp.int32, shape, 1)

    for c in range(rows // CHUNK):
        at = slice(c * CHUNK, (c + 1) * CHUNK)
        hit = cols_ref[at, 0:1] == lane_of((CHUNK, requests))
        picked = jnp.dot(
            jnp.where(hit, 1.0, 0.0).astype(jnp.bfloat16),
            q_ref[...],
            preferred_element_type=jnp.float32,
        )
        low, high = picked[:, :page_len], picked[:, page_len:]
        head = head_of((CHUNK, page_len))
        first = lane_of((CHUNK, page_len)) < half
        near = jnp.where(head == 0, low, pltpu.roll(low, half, 1))
        far = jnp.where(head == 2, pltpu.roll(high, half, 1), high)
        keep = first == (head < 2)
        qs[at, :] = jnp.where(keep, jnp.where(head < 2, near, far), 0.0).astype(jnp.bfloat16)

    quad_row = lax.broadcasted_iota(jnp.int32, (ROWS, page_len), 0) // HEADS

    def score(i, keys):
        q16 = qs[i * ROWS : (i + 1) * ROWS, :]
        wide = lax.dot_general(
            q16,
            keys.reshape(QUAD * page_len, page_len),
            (((1,), (1,)), ((), ())),
            preferred_element_type=jnp.float32,
        )
        got = wide[:, :page_len]
        for n in range(1, QUAD):
            got = jnp.where(quad_row == n, wide[:, n * page_len : (n + 1) * page_len], got)
        sc[i * ROWS : (i + 1) * ROWS, :] = got * SCORE_SCALE

    for c in range(SPLIT):
        arrive(c)
        for i in range(c * old_quads // SPLIT, (c + 1) * old_quads // SPLIT):
            score(i, k_ref[i * QUAD : (i + 1) * QUAD])

    arrive(SPLIT)
    for i in range(old_quads, quads):
        score(i, kn_ref[(i - old_quads) * QUAD : (i - old_quads + 1) * QUAD])

    tops, sums = [], []
    ceiling = jnp.full((8, requests), NEG_FILL, jnp.float32)
    for c in range(rows // CHUNK):
        at = slice(c * CHUNK, (c + 1) * CHUNK)
        valid = lane_of((CHUNK, page_len)) < cols_ref[at, 1:2]
        masked = jnp.where(valid, sc[at, :], NEG_FILL)
        top = jnp.max(masked, axis=1, keepdims=True)
        weight = jnp.where(valid, jnp.exp(masked - top), 0.0)
        sc[at, :] = weight
        tops.append(top)
        sums.append(jnp.sum(weight, axis=1, keepdims=True))
        hit = cols_ref[at, 0:1] == lane_of((CHUNK, requests))
        spread = jnp.where(hit, top, NEG_FILL).reshape(CHUNK // 8, 8, requests)
        ceiling = jnp.maximum(ceiling, jnp.max(spread, axis=0))
    ceiling = jnp.maximum(ceiling, pltpu.roll(ceiling, HEADS, 0))

    ob[rows:, :] = jnp.zeros((ob.shape[0] - rows, ob.shape[1]), ob.dtype)
    cb[rows:, :] = jnp.zeros((cb.shape[0] - rows, cb.shape[1]), cb.dtype)
    factors = []
    for c in range(rows // CHUNK):
        at = slice(c * CHUNK, (c + 1) * CHUNK)
        hit = cols_ref[at, 0:1] == lane_of((CHUNK, requests))
        limit = jnp.broadcast_to(ceiling[None], (CHUNK // 8, 8, requests))
        own = jnp.max(
            jnp.where(hit, limit.reshape(CHUNK, requests), NEG_FILL), axis=1, keepdims=True
        )
        factor = jnp.exp(tops[c] - own)
        factors.append(factor)
        lane = lane_of((CHUNK, page_len))
        leader = jnp.where(cols_ref[at, 2:3] > 0, own, 0.0)
        pieces = split_three(jnp.where(lane < 3 * HEADS, sums[c] * factor, leader))
        turn = (lane // HEADS) % 3
        stats = jnp.where(turn == 0, pieces[0], jnp.where(turn == 1, pieces[1], pieces[2]))
        keep = (lane % HEADS == head_of((CHUNK, page_len))) & (lane < 6 * HEADS)
        cb[at, :] = jnp.where(keep, stats, 0.0).astype(jnp.bfloat16)

    step = requests // 4

    def member(c):
        owner = lax.broadcasted_iota(jnp.int32, (step, ob.shape[0]), 0) + c * step
        return jnp.where(owner == req_ref[0:1, :], 1.0, 0.0).astype(jnp.bfloat16)

    for c in range(4):
        stats = jnp.dot(member(c), cb[...], preferred_element_type=jnp.float32)
        lane = lane_of((step, page_len))
        joined = (
            stats
            + pltpu.roll(stats, page_len - HEADS, 1)
            + pltpu.roll(stats, page_len - 2 * HEADS, 1)
        )
        high, middle, rest = split_three(joined)
        middle, rest = pltpu.roll(middle, HEADS, 1), pltpu.roll(rest, 2 * HEADS, 1)
        stats = jnp.where(lane < 3 * HEADS, rest, stats)
        stats = jnp.where(lane < 2 * HEADS, middle, stats)
        stats = jnp.where(lane < HEADS, high, stats)
        out_ref[c * step : (c + 1) * step, 2 * page_len :] = stats.astype(jnp.bfloat16)

    def blend(i, values):
        p16 = sc[i * ROWS : (i + 1) * ROWS, :]
        parts = [jnp.where(quad_row == n, p16, 0.0) for n in range(QUAD)]
        sc[i * ROWS : (i + 1) * ROWS, :] = jnp.dot(
            jnp.concatenate(parts, axis=1).astype(jnp.bfloat16),
            values.reshape(QUAD * page_len, page_len),
            preferred_element_type=jnp.float32,
        )

    for c in range(SPLIT):
        arrive(c + SPLIT + 1)
        for i in range(c * old_quads // SPLIT, (c + 1) * old_quads // SPLIT):
            blend(i, v_ref[i * QUAD : (i + 1) * QUAD])

    arrive(2 * SPLIT + 1)
    for i in range(old_quads, quads):
        blend(i, vn_ref[(i - old_quads) * QUAD : (i - old_quads + 1) * QUAD])

    for c in range(rows // CHUNK):
        at = slice(c * CHUNK, (c + 1) * CHUNK)
        value = sc[at, :] * factors[c]
        turned = pltpu.roll(value, half, 1)
        head = head_of((CHUNK, page_len))
        first = lane_of((CHUNK, page_len)) < half
        low = jnp.where(first, jnp.where(head == 0, value, 0.0), jnp.where(head == 1, turned, 0.0))
        high = jnp.where(first, jnp.where(head == 2, turned, 0.0), jnp.where(head == 3, value, 0.0))
        ob[at, :page_len] = low.astype(jnp.bfloat16)
        ob[at, page_len:] = high.astype(jnp.bfloat16)
    for c in range(4):
        total = jnp.dot(member(c), ob[...], preferred_element_type=jnp.float32)
        out_ref[c * step : (c + 1) * step, : 2 * page_len] = total.astype(jnp.bfloat16)


def attend(k_cache, v_cache, key_new, value_new, all_queries, columns, owner_row):
    slots = k_cache.shape[0] + key_new.shape[0]
    page_len, width = k_cache.shape[1:]
    rows = slots * HEADS
    padded = owner_row.shape[1]
    requests = all_queries.shape[0]
    return pl.pallas_call(
        attend_kernel,
        out_shape=jax.ShapeDtypeStruct((requests, 3 * width), jnp.bfloat16),
        in_specs=[pl.BlockSpec(memory_space=pltpu.HBM)] * 4
        + [pl.BlockSpec(memory_space=pltpu.VMEM)] * 3,
        out_specs=pl.BlockSpec(memory_space=pltpu.VMEM),
        scratch_shapes=[
            pltpu.VMEM(k_cache.shape, k_cache.dtype),
            pltpu.VMEM(v_cache.shape, v_cache.dtype),
            pltpu.VMEM(key_new.shape, key_new.dtype),
            pltpu.VMEM(value_new.shape, value_new.dtype),
            pltpu.VMEM((rows, width), jnp.bfloat16),
            pltpu.VMEM((rows, page_len), jnp.float32),
            pltpu.VMEM((padded, 2 * width), jnp.bfloat16),
            pltpu.VMEM((padded, width), jnp.bfloat16),
            pltpu.SemaphoreType.DMA((2 * SPLIT + 2,)),
        ],
        compiler_params=pltpu.CompilerParams(vmem_limit_bytes=59 << 20),
        cost_estimate=pl.CostEstimate(
            flops=4 * slots * ROWS * page_len * width * 4,
            bytes_accessed=4 * slots * page_len * width + (2 << 20),
            transcendentals=rows * page_len,
        ),
        name="attend",
    )(k_cache, v_cache, key_new, value_new, all_queries, columns, owner_row)


def call(kernel, outs, args, name, scratch=(), spaces=None, flops=0, limit=24 << 20):
    spaces = spaces or [pltpu.VMEM] * len(args)
    moved = sum(part.size * part.dtype.itemsize for part in list(args) + list(outs))
    return pl.pallas_call(
        kernel,
        out_shape=tuple(outs),
        in_specs=[pl.BlockSpec(memory_space=space) for space in spaces],
        out_specs=tuple(pl.BlockSpec(memory_space=pltpu.VMEM) for _ in outs),
        scratch_shapes=list(scratch),
        compiler_params=pltpu.CompilerParams(vmem_limit_bytes=limit),
        cost_estimate=pl.CostEstimate(flops=flops, bytes_accessed=moved, transcendentals=0),
        name=name,
    )(*args)


def query_kernel(tokens_ref, gain_ref, w_ref, out_ref):
    rows = rms_scale(tokens_ref[...].astype(jnp.float32), gain_ref[...].astype(jnp.float32))
    queries = jnp.dot(rows.astype(jnp.bfloat16), w_ref[...], preferred_element_type=jnp.float32)
    out_ref[...] = jnp.broadcast_to(queries.astype(jnp.bfloat16)[None], out_ref.shape)


def prepare_kernel(
    first_ref, hidden_hbm, table_hbm, lengths_ref, wk_hbm, wv_hbm,
    kn_ref, vn_ref, cols_ref, row_ref,
    hidden_ref, table_ref, turned, places, w_both, sems,
):
    part = hidden_ref.shape[0] // PARTS
    width = kn_ref.shape[1]
    copies = []
    early = (
        (table_hbm, table_ref),
        (wk_hbm, w_both.at[:, pl.ds(0, width)]),
        (wv_hbm, w_both.at[:, pl.ds(width, width)]),
    )
    first_copies = []
    for n, (whole, held) in enumerate(early):
        first_copies.append(pltpu.make_async_copy(whole, held, sems.at[PARTS + n]))
    for copy in first_copies:
        copy.start()
    for c in range(PARTS):
        at = pl.ds(c * part, part)
        copies.append(pltpu.make_async_copy(hidden_hbm.at[at], hidden_ref.at[at], sems.at[c]))
    for copy in copies:
        copy.start()
    slots, requests = places.shape
    page_len = turned.shape[0]
    lanes = 128
    first_copies[0].wait()
    ids = lax.broadcasted_iota(jnp.int32, (slots, lanes), 0) + first_ref[0]
    for g in range(requests // lanes):
        at = slice(g * lanes, (g + 1) * lanes)
        turned[:, at] = jnp.transpose(table_ref[at, :])
        longest = jnp.max(lengths_ref[g : g + 1, :].astype(jnp.float32)).astype(jnp.int32)

        def look(n, found, at=at):
            block = turned[pl.ds(pl.multiple_of(n * 8, 8), 8), at]
            for u in range(8):
                found = jnp.where(block[u : u + 1, :] == ids, n * 8 + u + 1, found)
            return found

        steps = (longest + 8 * page_len - 1) // (8 * page_len)
        places[:, at] = lax.fori_loop(0, steps, look, jnp.zeros((slots, lanes), jnp.int32))
    request = jnp.zeros((slots, 1), jnp.float32)
    limit = jnp.zeros((slots, 1), jnp.float32)
    leads = jnp.zeros((slots, 1), jnp.float32)
    slot = lax.broadcasted_iota(jnp.int32, (slots, lanes), 0)
    lane = lax.broadcasted_iota(jnp.int32, (slots, lanes), 1)

    def total(hit, value):
        return jnp.sum(jnp.where(hit, value.astype(jnp.float32), 0.0), axis=1, keepdims=True)

    for g in range(requests // lanes):
        place = places[:, g * lanes : (g + 1) * lanes]
        hit = place > 0
        request += total(hit, lane + g * lanes)
        limit += total(hit, lengths_ref[g : g + 1, :] - (place - 1) * page_len)
        order = jnp.where(hit, slot, slots).astype(jnp.float32)
        leads += total(hit & (order == jnp.min(order, axis=0, keepdims=True)), jnp.ones_like(lane))
    info = jnp.where(lane == 0, request, jnp.where(lane == 1, limit, leads)).astype(jnp.int32)
    rows = slots * HEADS
    cols_ref[rows:, :] = jnp.full((cols_ref.shape[0] - rows, lanes), -1, jnp.int32)
    for h in range(HEADS):
        cols_ref[pl.ds(h, slots, stride=HEADS), :] = info
    for c in range(cols_ref.shape[0] // lanes):
        at = slice(c * lanes, (c + 1) * lanes)
        row_ref[:, at] = jnp.transpose(cols_ref[at, :])[:8]
    for copy in first_copies[1:]:
        copy.wait()
    for c in range(PARTS):
        copies[c].wait()
        at = slice(c * part, (c + 1) * part)
        both = jnp.dot(hidden_ref[at, :], w_both[...], preferred_element_type=jnp.float32)
        kn_ref[at, :] = both[:, :width].astype(jnp.bfloat16)
        vn_ref[at, :] = both[:, width:].astype(jnp.bfloat16)


def join_kernel(landed_ref, w_ref, out_ref):
    sources, owned, wide = landed_ref.shape
    lanes = wide // 3
    stats = landed_ref[:, :, 2 * lanes :].astype(jnp.float32).reshape(sources * owned, lanes)
    stats = (
        stats + pltpu.roll(stats, lanes - HEADS, 1) + pltpu.roll(stats, lanes - 2 * HEADS, 1)
    )
    lane = lax.broadcasted_iota(jnp.int32, stats.shape, 1)
    sums = jnp.where(lane < HEADS, stats, 0.0)
    tops = jnp.where(sums > 0.0, pltpu.roll(stats, lanes - 3 * HEADS, 1), NEG_FILL)
    tops = tops.reshape(sources, owned, lanes)
    weights = jnp.exp(tops - jnp.max(tops, axis=0, keepdims=True))
    totals = jnp.sum(weights * sums.reshape(sources, owned, lanes), axis=0)
    lane = lax.broadcasted_iota(jnp.int32, (1, lanes), 1)
    weights = weights.reshape(sources * owned, lanes)

    def spread(value, n):
        return jnp.where(lane < lanes // 2, value[:, 2 * n : 2 * n + 1], value[:, 2 * n + 1 : 2 * n + 2])

    projected = jnp.zeros(out_ref.shape, jnp.float32)
    for n in range(2):
        at = slice(n * lanes, (n + 1) * lanes)
        value = landed_ref[:, :, at].astype(jnp.float32).reshape(sources * owned, lanes)
        value = jnp.sum((value * spread(weights, n)).reshape(sources, owned, lanes), axis=0)
        attended = (value / spread(totals, n)).astype(jnp.bfloat16)
        projected += jnp.dot(attended, w_ref[at, :], preferred_element_type=jnp.float32)
    out_ref[...] = projected


def dispatch_kernel(tokens_ref, gain_ref, send_ref, *refs):
    *share_refs, mixed_ref, out_ref = refs
    mixed = tokens_ref[...].astype(jnp.float32) + sum(share[...].astype(jnp.float32) for share in share_refs)
    mixed_ref[...] = mixed
    normed = rms_scale(mixed, gain_ref[...].astype(jnp.float32)).astype(jnp.bfloat16)
    out_ref[...] = jnp.dot(send_ref[...], normed, preferred_element_type=jnp.float32).astype(
        jnp.bfloat16
    )


def expert_kernel(rows_ref, gate_ref, up_ref, down_ref, out_ref):
    rows = rows_ref[...]
    gate = jnp.dot(rows, gate_ref[...], preferred_element_type=jnp.float32)
    up = jnp.dot(rows, up_ref[...], preferred_element_type=jnp.float32)
    hidden = (gate / (1.0 + jnp.exp(-gate)) * up).astype(jnp.bfloat16)
    out_ref[...] = jnp.dot(hidden, down_ref[...], preferred_element_type=jnp.float32).astype(
        jnp.bfloat16
    )


def rms_scale(row_vals, gain_row):
    mean_sq = jnp.mean(row_vals * row_vals, axis=-1, keepdims=True)
    return row_vals * lax.rsqrt(mean_sq + EPSILON) * gain_row


def on_device(
    tokens,
    block_table,
    lengths,
    k_cache,
    v_cache,
    hidden_store,
    norm_attn,
    w_query,
    w_key,
    w_value,
    w_out,
    norm_moe,
    expert_ids,
    gate_weights,
    w_gate,
    w_up,
    w_down,
):
    pool_count = lax.axis_size("pool")
    exp_count = lax.axis_size("exp")
    pool_index = lax.axis_index("pool")
    exp_index = lax.axis_index("exp")
    req_dev = tokens.shape[0]
    model_width = tokens.shape[1]
    quarter = model_width // exp_count
    bf16 = jnp.bfloat16
    query_width = w_query.shape[1]
    head_count = query_width // HEAD_SIZE
    (copies,) = call(
        query_kernel,
        [jax.ShapeDtypeStruct((pool_count, req_dev, query_width), bf16)],
        [tokens, norm_attn, w_query],
        "query",
        limit=60 << 20,
    )
    all_queries = lax.all_to_all(copies, "pool", split_axis=0, concat_axis=0, tiled=True)
    all_queries = all_queries.reshape(-1, query_width)
    slot_count = k_cache.shape[0] + hidden_store.shape[0]
    page_len, key_width = k_cache.shape[1:]
    requests = block_table.shape[0]
    stored_rows = hidden_store.reshape(-1, model_width)
    padded = -(-slot_count * head_count // 128) * 128
    key_new, value_new, columns, owner_row = call(
        prepare_kernel,
        [jax.ShapeDtypeStruct((stored_rows.shape[0], key_width), bf16)] * 2
        + [
            jax.ShapeDtypeStruct((padded, 128), jnp.int32),
            jax.ShapeDtypeStruct((8, padded), jnp.int32),
        ],
        [
            jnp.full((1,), pool_index * slot_count, jnp.int32),
            stored_rows,
            block_table,
            lengths.reshape(-1, 128),
            w_key,
            w_value,
        ],
        "prepare",
        [
            pltpu.VMEM(stored_rows.shape, bf16),
            pltpu.VMEM(block_table.shape, jnp.int32),
            pltpu.VMEM((block_table.shape[1], requests), jnp.int32),
            pltpu.VMEM((slot_count, requests), jnp.int32),
            pltpu.VMEM((model_width, 2 * key_width), bf16),
            pltpu.SemaphoreType.DMA((PARTS + 3,)),
        ],
        [pltpu.SMEM, pltpu.HBM, pltpu.HBM, pltpu.VMEM, pltpu.HBM, pltpu.HBM],
        4 * stored_rows.size * key_width,
        60 << 20,
    )
    key_new = key_new.reshape(-1, page_len, key_width)
    value_new = value_new.reshape(-1, page_len, key_width)
    parcel = attend(k_cache, v_cache, key_new, value_new, all_queries, columns, owner_row)
    parcel, w_down = lax.optimization_barrier((parcel, w_down))
    down_share = lax.dynamic_slice_in_dim(w_down[0], exp_index * quarter, quarter, 1)
    parcel = parcel.reshape(pool_count, req_dev, -1)
    landed = lax.all_to_all(parcel, "pool", split_axis=0, concat_axis=0, tiled=True)
    (projected,) = call(
        join_kernel,
        [jax.ShapeDtypeStruct((req_dev, model_width), jnp.float32)],
        [landed, w_out],
        "join",
    )
    projected, expert_ids = lax.optimization_barrier((projected, expert_ids))
    shares = [projected] + others(projected.astype(bf16), "exp")
    top_count = expert_ids.shape[1]
    capacity = min(req_dev, 2 * ((req_dev * top_count + pool_count - 1) // pool_count))
    route_flat = expert_ids.reshape(-1)
    expert_hit = (route_flat[:, None] == jnp.arange(pool_count, dtype=jnp.int32)[None, :]).astype(
        jnp.int32
    )
    slot_rank = jnp.sum(jnp.cumsum(expert_hit, axis=0) * expert_hit, axis=1) - 1
    slot_pos = route_flat * capacity + slot_rank
    placed = (
        slot_pos[:, None] == jnp.arange(pool_count * capacity, dtype=jnp.int32)[None, :]
    ).astype(jnp.float32)
    placed = placed.reshape(req_dev, top_count, pool_count * capacity)
    send_map = jnp.sum(placed, axis=1).astype(jnp.bfloat16)
    combine_map = jnp.einsum("tk,tkc->tc", gate_weights, placed, precision=HIGHEST)
    mixed, outgoing = call(
        dispatch_kernel,
        [
            jax.ShapeDtypeStruct((req_dev, model_width), jnp.float32),
            jax.ShapeDtypeStruct((pool_count * capacity, model_width), bf16),
        ],
        [tokens, norm_moe, send_map.T] + shares,
        "dispatch",
    )
    outgoing = outgoing.reshape(pool_count, capacity, model_width)
    arrived = lax.all_to_all(outgoing, "pool", split_axis=0, concat_axis=0, tiled=True)
    sources = arrived.shape[0]
    slots_here = arrived.shape[1]
    row_block = arrived.reshape(-1, model_width)
    (expert_low,) = call(
        expert_kernel,
        [jax.ShapeDtypeStruct((row_block.shape[0], quarter), bf16)],
        [row_block, w_gate[0], w_up[0], down_share],
        "expert",
        flops=4 * row_block.size * w_up.shape[2],
        limit=16 << 20,
    )
    expert_out = expert_low.reshape(sources, slots_here, quarter)
    returned = lax.all_to_all(expert_out, "pool", split_axis=0, concat_axis=0, tiled=True)
    moe_share = jnp.dot(
        combine_map,
        returned.reshape(pool_count * capacity, quarter).astype(jnp.float32),
        precision=HIGHEST,
    )
    mixed_share = lax.dynamic_slice_in_dim(mixed, exp_index * quarter, quarter, 1)
    return (mixed_share + moe_share).astype(jnp.bfloat16)


def solution(mesh):
    placed = (
        P("pool", None),
        P(),
        P(),
        P("pool", None, "exp"),
        P("pool", None, "exp"),
        P("pool", None, None),
        P(),
        P(None, "exp"),
        P(None, "exp"),
        P(None, "exp"),
        P("exp", None),
        P(),
        P("pool", None),
        P("pool", None),
        P("pool", None, None),
        P("pool", None, None),
        P("pool", None, None),
    )
    return jax.shard_map(
        on_device, mesh=mesh, in_specs=placed, out_specs=P("pool", "exp"), check_vma=False
    )
```
